32 devices in a mesh: lat: 4 (over y, x), lon: 8 (over z, core).
Axes of the slice: x: 2, y: 2, z: 4, core: 2. Of those that a mesh axis runs over, the one named last changes fastest.
Arguments:
- frame_one: bfloat16 [64, 256, 256], P('lat', 'lon'), may hold values from -6 to 6
- frame_two: bfloat16 [64, 256, 256], P('lat', 'lon'), may hold values from -6 to 6
- enc_weight: bfloat16 [3, 3, 256, 256], replicated, may hold values from -0.125 to 0.125
- mask_weight: bfloat16 [256, 576], replicated, may hold values from -0.375 to 0.375
Outputs:
- up_flow: float32 [2, 512, 2048], P(None, 'lat', 'lon')
The draws below stay inside these ranges and needn't reach their ends.
All inputs are finite; a program needn't handle non-finite values.
Results may differ from the reference program's by a relative error of at most 0.0011.
Values may be sent and summed in bfloat16 or wider, within the bound.
A program may use at most 64 MiB of HBM per device.

```python
import math
import jax
import jax.numpy as jnp
from jax import lax

CHANNELS = 256
BLOCK_ROWS = 8
BLOCK_COLS = 16
UPSCALE = 8
MASK_COLS = 576
GRID_ROWS = 64
GRID_COLS = 256


def level_of(rng, extent, cuts, low, largest):
    def one(axis_at, blocks):
        draws = jax.random.uniform(jax.random.fold_in(jax.random.fold_in(rng, 6), axis_at), (blocks,), jnp.float32, low / len(cuts), largest / len(cuts))
        return jnp.repeat(jnp.exp(draws), extent[axis_at] // blocks).reshape((-1,) + (1,) * (len(extent) - axis_at - 1))

    gain = one(*cuts[0])
    for cut in cuts[1:]:
        gain = gain * one(*cut)
    return gain


def scatter_about(own_key, extent, scale, reach, split=(), kind=jnp.bfloat16):
    result = jax.random.normal(own_key, extent, jnp.float32) * scale
    if len(split) > 0:
        result = level_of(own_key, extent, split, -0.22, 0.18) * result
    return jnp.clip(result, min=-reach, max=reach).astype(kind)


def setup_inputs(seed: int = 0) -> dict:
    streams_of = jax.random.split(jax.random.key(seed), 5)
    frame_one = scatter_about(streams_of[0], (GRID_ROWS, GRID_COLS, CHANNELS), 1.0, 6.0, ((0, 4), (1, 8)))
    frame_two = scatter_about(streams_of[1], (GRID_ROWS, GRID_COLS, CHANNELS), 1.0, 6.0, ((0, 4), (1, 8)))
    enc_weight = scatter_about(streams_of[2], (3, 3, CHANNELS, CHANNELS), (9 * CHANNELS) ** -0.5, 0.125)
    mask_weight = scatter_about(streams_of[3], (CHANNELS, MASK_COLS), CHANNELS ** -0.5, 0.375)
    return dict(frame_one=frame_one, frame_two=frame_two, enc_weight=enc_weight, mask_weight=mask_weight)


def encode_grid(source, weight):
    padded = jnp.pad(source, ((1, 1), (0, 0), (0, 0)))
    summed = jnp.zeros((GRID_ROWS, GRID_COLS, CHANNELS), jnp.float32)
    for row_off in range(3):
        for col_off in range(3):
            moved = jnp.roll(padded[row_off:row_off + GRID_ROWS], 1 - col_off, axis=1)
            summed = summed + jnp.dot(moved.reshape(GRID_ROWS * GRID_COLS, CHANNELS), weight[row_off, col_off], preferred_element_type=jnp.float32).reshape(GRID_ROWS, GRID_COLS, CHANNELS)
    return summed.astype(jnp.bfloat16)

def reference(frame_one, frame_two, enc_weight, mask_weight):
    enc_one = encode_grid(frame_one, enc_weight)
    enc_two = encode_grid(frame_two, enc_weight)
    padded_two = jnp.pad(enc_two, ((BLOCK_ROWS, BLOCK_ROWS), (0, 0), (0, 0)))
    block_size = BLOCK_ROWS * BLOCK_COLS
    column_blocks = GRID_COLS // BLOCK_COLS
    row_blocks = GRID_ROWS // BLOCK_ROWS
    key_row = (jnp.arange(block_size) // BLOCK_COLS).astype(jnp.float32)
    key_col = (jnp.arange(block_size) % BLOCK_COLS).astype(jnp.float32)
    scale = 1.0 / math.sqrt(CHANNELS)

    def block_row(index):
        query = lax.dynamic_slice_in_dim(enc_one, index * BLOCK_ROWS, BLOCK_ROWS, 0)
        query = query.reshape(BLOCK_ROWS, column_blocks, BLOCK_COLS, CHANNELS).transpose(1, 0, 2, 3)
        query = query.reshape(column_blocks, block_size, CHANNELS).astype(jnp.float32)
        window = lax.dynamic_slice_in_dim(padded_two, index * BLOCK_ROWS, 3 * BLOCK_ROWS, 0)
        window = window.reshape(3, BLOCK_ROWS, column_blocks, BLOCK_COLS, CHANNELS).transpose(0, 2, 1, 3, 4)
        window = window.reshape(3, column_blocks, block_size, CHANNELS).astype(jnp.float32)
        mass = jnp.zeros((column_blocks, block_size), jnp.float32)
        sum_y = jnp.zeros((column_blocks, block_size), jnp.float32)
        sum_x = jnp.zeros((column_blocks, block_size), jnp.float32)
        for row_off in range(3):
            target = index + row_off - 1
            inside = ((target >= 0) & (target < row_blocks)).astype(jnp.float32)
            for col_off in range(3):
                keyed = jnp.roll(window[row_off], 1 - col_off, axis=0)
                scores = jnp.einsum('jqc,jkc->jqk', query, keyed) * scale
                expo = jnp.exp(scores) * inside
                part = lax.optimization_barrier(jnp.sum(expo, axis=-1))
                mass = mass + part
                sum_y = sum_y + lax.optimization_barrier(jnp.sum(expo * key_row, axis=-1)) + BLOCK_ROWS * (row_off - 1) * part
                sum_x = sum_x + lax.optimization_barrier(jnp.sum(expo * key_col, axis=-1)) + BLOCK_COLS * (col_off - 1) * part
        flow_y = sum_y / mass - key_row
        flow_x = sum_x / mass - key_col
        stacked = jnp.stack([flow_y, flow_x]).reshape(2, column_blocks, BLOCK_ROWS, BLOCK_COLS)
        return stacked.transpose(0, 2, 1, 3).reshape(2, BLOCK_ROWS, GRID_COLS)
    rows_out = lax.map(block_row, jnp.arange(row_blocks, dtype=jnp.int32))
    flow = rows_out.transpose(1, 0, 2, 3).reshape(2, GRID_ROWS, GRID_COLS)
    logits = jnp.dot(enc_one.reshape(GRID_ROWS * GRID_COLS, CHANNELS), mask_weight, preferred_element_type=jnp.float32)
    logits = logits.reshape(GRID_ROWS, GRID_COLS, 9, UPSCALE * UPSCALE)
    expo = jnp.exp(logits)
    mix = expo / lax.optimization_barrier(jnp.sum(expo, axis=2, keepdims=True))
    padded_flow = jnp.pad(flow, ((0, 0), (1, 1), (0, 0)))
    upsampled = jnp.zeros((2, GRID_ROWS, GRID_COLS, UPSCALE * UPSCALE), jnp.float32)
    for row_off in range(3):
        for col_off in range(3):
            beside = jnp.roll(padded_flow[:, row_off:row_off + GRID_ROWS], 1 - col_off, axis=2) * UPSCALE
            upsampled = upsampled + mix[None, :, :, 3 * row_off + col_off, :] * beside[..., None]
    upsampled = upsampled.reshape(2, GRID_ROWS, GRID_COLS, UPSCALE, UPSCALE).transpose(0, 1, 3, 2, 4)
    return upsampled.reshape(2, GRID_ROWS * UPSCALE, GRID_COLS * UPSCALE)
```

```python
import functools
import math

import jax
import jax.numpy as jnp
from jax import lax
from jax.experimental import pallas as pl
from jax.experimental.pallas import tpu as pltpu
from jax.sharding import PartitionSpec as P

BLOCK_ROWS = 8
BLOCK_COLS = 16
BLOCK = BLOCK_ROWS * BLOCK_COLS
UPSCALE = 8
F32 = jnp.float32
BF16 = jnp.bfloat16
MESH = pl.DeviceIdType.MESH


def iota(shape, axis):
    return lax.broadcasted_iota(jnp.int32, shape, axis)


def mm(a, b):
    return jnp.dot(a, b, preferred_element_type=F32)


def mm_nt(a, b):
    return lax.dot_general(a, b, (((1,), (1,)), ((), ())), preferred_element_type=F32)


def swap_groups(xs, lane_group):
    xs = list(xs)
    for bit in (1, 2, 4):
        mask = (lane_group & bit) != 0
        shift = bit * BLOCK_COLS
        for a in range(8):
            if a & bit:
                continue
            lo, hi = xs[a], xs[a | bit]
            xs[a] = jnp.where(mask, pltpu.roll(hi, shift, 1), lo)
            xs[a | bit] = jnp.where(mask, hi, pltpu.roll(lo, BLOCK - shift, 1))
    return xs


def kernel(
    f1, f2, w_hbm, mw_hbm, out,
    fr, wv, mv, wp, acc, hal, strip_s, strip_r, corner_s, corner_r, keys, qs, mix, fb,
    lsem, ssem, rsem,
):
    rows, cols, ch = f1.shape
    rb_n, cb_n = rows // BLOCK_ROWS, cols // BLOCK_COLS
    n_mask = mw_hbm.shape[1]
    lat, lon = lax.axis_index("lat"), lax.axis_index("lon")
    nlat, nlon = lax.axis_size("lat"), lax.axis_size("lon")
    has_n, has_s = lat > 0, lat < nlat - 1
    left = (lat, lax.rem(lon + nlon - 1, nlon))
    right = (lat, lax.rem(lon + 1, nlon))
    north, south = (lat - 1, lon), (lat + 1, lon)

    loads = [
        pltpu.make_async_copy(f1, fr.at[0, pl.ds(1, rows)], lsem.at[0]),
        pltpu.make_async_copy(f2, fr.at[1, pl.ds(1, rows)], lsem.at[1]),
        pltpu.make_async_copy(w_hbm, wv, lsem.at[2]),
        pltpu.make_async_copy(mw_hbm, mv, lsem.at[3]),
    ]
    for load in loads:
        load.start()

    barrier = pltpu.get_barrier_semaphore()

    def greet(peer):
        pl.semaphore_signal(barrier, inc=1, device_id=peer, device_id_type=MESH)

    greet(left)
    greet(right)
    pl.when(has_n)(lambda: greet(north))
    pl.when(has_s)(lambda: greet(south))

    def send(k, src, dst, peer):
        return pltpu.make_async_remote_copy(
            src_ref=src, dst_ref=dst, send_sem=ssem.at[k], recv_sem=rsem.at[k],
            device_id=peer, device_id_type=MESH,
        )

    zero_row = jnp.zeros((cols, ch), BF16)
    for f in range(2):
        fr[f, 0] = zero_row
        fr[f, rows + 1] = zero_row

    halo_rows = {
        0: [send(0, f1.at[0], hal.at[1, 0], north), send(1, f2.at[0], hal.at[1, 1], north)],
        1: [
            send(2, f1.at[rows - 1], hal.at[0, 0], south),
            send(3, f2.at[rows - 1], hal.at[0, 1], south),
        ],
    }
    strips = [
        send(4, strip_s.at[0], strip_r.at[1], left),
        send(5, strip_s.at[1], strip_r.at[0], right),
    ]
    corners = [
        send(6, corner_s.at[0], corner_r.at[1], left),
        send(7, corner_s.at[1], corner_r.at[0], right),
    ]

    def absent(side):
        return jnp.logical_not(has_n if side == 0 else has_s)

    def present(side):
        return has_n if side == 0 else has_s

    for side in range(2):

        @pl.when(absent(side))
        def _():
            hal[side] = jnp.zeros(hal.shape[1:], hal.dtype)
            lo = 0 if side == 0 else BLOCK_ROWS + rows
            keys[lo : lo + BLOCK_ROWS] = jnp.zeros((BLOCK_ROWS,) + keys.shape[1:], BF16)
            at = 0 if side == 0 else rb_n + 1
            fb[at] = jnp.zeros(fb.shape[1:], F32)

    loads[0].wait()
    loads[1].wait()
    for side in range(2):
        lo, pick = (0, 0) if side == 0 else (cols - 16, 15)
        for f in range(2):
            tile = fr[f, 1 : rows + 1, lo : lo + 16, :].astype(F32)
            one = jnp.sum(jnp.where(iota(tile.shape, 1) == pick, tile, 0.0), axis=1)
            strip_s[side, f * rows : (f + 1) * rows] = one.astype(BF16)

    pl.semaphore_wait(barrier, 2 + has_n.astype(jnp.int32) + has_s.astype(jnp.int32))

    for side in range(2):

        @pl.when(present(side))
        def _():
            for copy in halo_rows[side]:
                copy.start()

    for copy in strips:
        copy.start()

    loads[2].wait()

    def col_shift(y, side):
        flat = y.reshape(-1, ch)
        n = flat.shape[0]
        turned = pltpu.roll(flat, 1 if side == 0 else n - 1, 0).reshape(y.shape)
        edge = 0 if side == 0 else cols - 1
        return jnp.where(iota(y.shape, 1) == edge, 0.0, turned)

    for f in range(2):
        lhs = jnp.concatenate(
            [fr[f, a : a + rows].reshape(rows * cols, ch) for a in range(3)], axis=1
        )
        ys = [mm(lhs, wv[:, b].reshape(3 * ch, ch)).reshape(rows, cols, ch) for b in range(3)]
        acc[f] = ys[1] + col_shift(ys[0], 0) + col_shift(ys[2], 1)

    for side in range(2):

        @pl.when(present(side))
        def _():
            for copy in halo_rows[1 - side]:
                copy.wait_recv()

    for side in range(2):
        edge = 0 if side == 0 else cols - 1
        base = 0 if side == 0 else cols - 16
        got = jnp.zeros((16, ch), F32)
        for f in range(2):
            for end in range(2):
                tile = hal[end, f, base : base + 16, :].astype(F32)
                one = tile[edge - base : edge - base + 1]
                got = jnp.where(iota((16, ch), 0) == 2 * f + end, one, got)
        corner_s[side] = got.astype(BF16)
    for copy in corners:
        copy.start()

    for side in range(2):
        a = 0 if side == 0 else 2
        r = 0 if side == 0 else rows - 1
        flat = hal[side].reshape(2 * cols, ch)
        ys = [mm(flat, wv[a, b]).reshape(2, cols, ch) for b in range(3)]
        y = ys[1] + col_shift(ys[0], 0) + col_shift(ys[2], 1)
        for f in range(2):
            acc[f, r] = acc[f, r] + y[f]

    loads[3].wait()
    p = iota((n_mask, n_mask), 0)
    want = (p - (p & 63)) + ((p & 7) << 3) + ((p >> 3) & 7)
    perm = (iota((n_mask, n_mask), 1) == want).astype(F32).astype(BF16)
    wp[...] = mm_nt(perm, mv[...]).astype(BF16)

    for copy in strips + corners:
        copy.wait_recv()
    row_id = iota((rows, ch), 0)
    for side in range(2):
        b = 0 if side == 0 else 2
        lhs = jnp.concatenate([strip_r[side], corner_r[side]], axis=0)
        z = [mm(lhs, wv[a, b]) for a in range(3)]
        for f in range(2):
            own = [z[a][f * rows : (f + 1) * rows] for a in range(3)]
            top = z[0][2 * rows + 2 * f : 2 * rows + 2 * f + 1]
            bottom = z[2][2 * rows + 2 * f + 1 : 2 * rows + 2 * f + 2]
            h = own[1] + jnp.where(row_id == 0, top, pltpu.roll(own[0], 1, 0))
            h = h + jnp.where(row_id == rows - 1, bottom, pltpu.roll(own[2], rows - 1, 0))
            lo, pick = (0, 0) if side == 0 else (cols - 8, 7)
            tile = acc[f, :, lo : lo + 8, :]
            acc[f, :, lo : lo + 8, :] = tile + jnp.where(
                iota(tile.shape, 1) == pick, h[:, None, :], 0.0
            )

    own_r = pl.ds(BLOCK_ROWS, rows)
    own_c = pl.ds(BLOCK_COLS, cols)
    keys[BLOCK_ROWS : BLOCK_ROWS + rows, BLOCK_COLS : BLOCK_COLS + cols] = acc[1].astype(BF16)

    br, bc = BLOCK_ROWS, BLOCK_COLS
    key_rows = [
        send(8, keys.at[pl.ds(br, br), own_c], keys.at[pl.ds(br + rows, br), own_c], north),
        send(9, keys.at[pl.ds(rows, br), own_c], keys.at[pl.ds(0, br), own_c], south),
    ]
    first, last = pl.ds(bc, bc), pl.ds(cols, bc)
    to_left, to_right = pl.ds(bc + cols, bc), pl.ds(0, bc)
    key_cols = [
        send(10, keys.at[own_r, first], keys.at[own_r, to_left], left),
        send(11, keys.at[own_r, last], keys.at[own_r, to_right], right),
    ]
    key_corners = {}
    for side in range(2):
        r = pl.ds(0 if side == 0 else br + rows, br)
        key_corners[side] = [
            send(12 + 2 * side, keys.at[r, first], keys.at[r, to_left], left),
            send(13 + 2 * side, keys.at[r, last], keys.at[r, to_right], right),
        ]
    for side in range(2):

        @pl.when(present(side))
        def _():
            key_rows[side].start()

    for copy in key_cols:
        copy.start()

    for cb in range(cb_n):
        for rb in range(rb_n):
            block = acc[0, rb * br : (rb + 1) * br, cb * bc : (cb + 1) * bc, :]
            qs[cb, rb * BLOCK : (rb + 1) * BLOCK] = block.astype(BF16).reshape(BLOCK, ch)

    scale = 1.0 / math.sqrt(ch)
    inside = [has_n.astype(F32), has_s.astype(F32)]
    zero = jnp.zeros((8, BLOCK), F32)
    totals = {(rb, cb): [zero, zero, zero] for rb in range(rb_n) for cb in range(cb_n)}
    sub = iota((8, BLOCK), 0).astype(F32)

    def correlate(kbs, kc):
        part = keys[kbs[0] * br : (kbs[-1] + 1) * br, kc * bc : (kc + 1) * bc, :]
        part = part.reshape(len(kbs) * BLOCK, ch)
        for cb in range(max(0, kc - 2), min(cb_n, kc + 1)):
            rbs = [rb for rb in range(rb_n) if any(0 <= kb - rb <= 2 for kb in kbs)]
            r0 = rbs[0]
            s = mm_nt(part, qs[cb, r0 * BLOCK : (rbs[-1] + 1) * BLOCK])
            for at, kb in enumerate(kbs):
                for rb in rbs:
                    if not 0 <= kb - rb <= 2:
                        continue
                    e = s[at * BLOCK : (at + 1) * BLOCK, (rb - r0) * BLOCK : (rb - r0 + 1) * BLOCK]
                    e = jnp.exp(e * scale).reshape(br, 2, 8, BLOCK)
                    lanes = [e[:, h] for h in range(2)]
                    by_row = lanes[0] + lanes[1]
                    y = by_row[0] * float(br * (kb - rb - 1))
                    for kr in range(1, br):
                        y = y + by_row[kr] * float(br * (kb - rb - 1) + kr)
                    by_col = [jnp.sum(h, axis=0) for h in lanes]
                    m = by_col[0] + by_col[1]
                    off = float(bc * (kc - cb - 1))
                    x = by_col[0] * (sub + off) + by_col[1] * (sub + (off + 8.0))
                    if kb == 0 or kb == rb_n + 1:
                        gate = inside[0] if kb == 0 else inside[1]
                        m, y, x = m * gate, y * gate, x * gate
                    old = totals[rb, cb]
                    totals[rb, cb] = [old[0] + m, old[1] + y, old[2] + x]

    own_kbs = list(range(1, rb_n + 1))
    for kc in range(1, cb_n + 1):
        correlate(own_kbs, kc)

    for cb in range(cb_n):
        logits = mm_nt(wp[...], qs[cb]).reshape(9, UPSCALE * UPSCALE, rb_n * BLOCK)
        e = jnp.exp(logits)
        mix[cb] = e / jnp.sum(e, axis=0, keepdims=True)

    for side in range(2):

        @pl.when(present(side))
        def _():
            key_rows[1 - side].wait_recv()
            for copy in key_corners[side]:
                copy.start()

    for kc in range(1, cb_n + 1):
        correlate([0], kc)
        correlate([rb_n + 1], kc)
    for copy in key_cols:
        copy.wait_recv()
    for kc in (0, cb_n + 1):
        correlate(own_kbs, kc)
    for side in range(2):

        @pl.when(present(side))
        def _():
            for copy in key_corners[side]:
                copy.wait_recv()

    for kc in (0, cb_n + 1):
        correlate([0], kc)
        correlate([rb_n + 1], kc)

    lane = iota((8, BLOCK), 1)
    sublane = iota((8, BLOCK), 0)
    qr, qc = lane >> 4, lane & 15
    for (rb, cb), (m, y, x) in totals.items():
        m, y, x = [jnp.sum(t, axis=0, keepdims=True) for t in (m, y, x)]
        fy = y / m - qr.astype(F32)
        fx = x / m - qc.astype(F32)
        both = jnp.where(sublane == 0, fy, fx) * float(UPSCALE)
        fb[rb + 1, cb + 1] = both

    flow_rows = [
        send(16, fb.at[1, pl.ds(1, cb_n)], fb.at[rb_n + 1, pl.ds(1, cb_n)], north),
        send(17, fb.at[rb_n, pl.ds(1, cb_n)], fb.at[0, pl.ds(1, cb_n)], south),
    ]
    flow_cols = [
        send(18, fb.at[pl.ds(1, rb_n), 1], fb.at[pl.ds(1, rb_n), cb_n + 1], left),
        send(19, fb.at[pl.ds(1, rb_n), cb_n], fb.at[pl.ds(1, rb_n), 0], right),
    ]
    flow_corners = {}
    for side in range(2):
        r = 0 if side == 0 else rb_n + 1
        flow_corners[side] = [
            send(20 + 2 * side, fb.at[r, 1], fb.at[r, cb_n + 1], left),
            send(21 + 2 * side, fb.at[r, cb_n], fb.at[r, 0], right),
        ]
    for side in range(2):

        @pl.when(present(side))
        def _():
            flow_rows[side].start()

    for copy in flow_cols:
        copy.start()
    for side in range(2):

        @pl.when(present(side))
        def _():
            flow_rows[1 - side].wait_recv()
            for copy in flow_corners[side]:
                copy.start()

    for copy in flow_cols:
        copy.wait_recv()
    for side in range(2):

        @pl.when(present(side))
        def _():
            for copy in flow_corners[side]:
                copy.wait_recv()

    k = iota((BLOCK, BLOCK), 0)
    weave = (iota((BLOCK, BLOCK), 1) == ((k & 15) << 3) + (k >> 4)).astype(F32).astype(BF16)

    for cb in range(cb_n):
        for rb in range(rb_n):
            shifted = {}
            for r in range(rb, rb + 3):
                mid = fb[r, cb + 1]
                shifted[r, 0] = jnp.where(
                    qc == 0, pltpu.roll(fb[r, cb], BLOCK - 15, 1), pltpu.roll(mid, 1, 1)
                )
                shifted[r, 1] = mid
                shifted[r, 2] = jnp.where(
                    qc == 15, pltpu.roll(fb[r, cb + 2], 15, 1), pltpu.roll(mid, BLOCK - 1, 1)
                )
            beside = []
            for a in range(3):
                for b in range(3):
                    here = shifted[rb + 1, b]
                    if a == 0:
                        here = pltpu.roll(jnp.where(qr == 7, shifted[rb, b], here), bc, 1)
                    if a == 2:
                        here = pltpu.roll(
                            jnp.where(qr == 0, shifted[rb + 2, b], here), BLOCK - bc, 1
                        )
                    beside.append(here)
            for d in range(2):
                up = jnp.zeros((UPSCALE * UPSCALE, BLOCK), F32)
                for n in range(9):
                    share = mix[cb, n, :, rb * BLOCK : (rb + 1) * BLOCK]
                    up = up + share * beside[n][d : d + 1]
                xs = [up[8 * j : 8 * j + 8] for j in range(8)]
                rowed = jnp.concatenate(swap_groups(xs, qr), axis=0)
                high = rowed.astype(BF16)
                rest = rowed - high.astype(F32)
                mid = rest.astype(BF16)
                low = (rest - mid.astype(F32)).astype(BF16)
                woven = mm(high, weave) + mm(mid, weave) + mm(low, weave)
                out[d, rb * 64 : (rb + 1) * 64, cb * BLOCK : (cb + 1) * BLOCK] = woven

    for side in range(2):

        @pl.when(present(side))
        def _():
            for copy in halo_rows[side] + [key_rows[side], flow_rows[side]]:
                copy.wait_send()
            for copy in key_corners[side] + flow_corners[side]:
                copy.wait_send()

    for copy in strips + corners + key_cols + flow_cols:
        copy.wait_send()


def body(frame_one, frame_two, enc_weight, mask_weight):
    rows, cols, ch = frame_one.shape
    n_mask = mask_weight.shape[1]
    rb_n, cb_n = rows // BLOCK_ROWS, cols // BLOCK_COLS
    return pl.pallas_call(
        kernel,
        out_shape=jax.ShapeDtypeStruct((2, rows * UPSCALE, cols * UPSCALE), F32),
        in_specs=[pl.BlockSpec(memory_space=pl.ANY)] * 4,
        out_specs=pl.BlockSpec(memory_space=pltpu.VMEM),
        scratch_shapes=[
            pltpu.VMEM((2, rows + 2, cols, ch), BF16),
            pltpu.VMEM(enc_weight.shape, BF16),
            pltpu.VMEM(mask_weight.shape, BF16),
            pltpu.VMEM((n_mask, ch), BF16),
            pltpu.VMEM((2, rows, cols, ch), F32),
            pltpu.VMEM((2, 2, cols, ch), BF16),
            pltpu.VMEM((2, 2 * rows, ch), BF16),
            pltpu.VMEM((2, 2 * rows, ch), BF16),
            pltpu.VMEM((2, 16, ch), BF16),
            pltpu.VMEM((2, 16, ch), BF16),
            pltpu.VMEM((rows + 2 * BLOCK_ROWS, cols + 2 * BLOCK_COLS, ch), BF16),
            pltpu.VMEM((cb_n, rb_n * BLOCK, ch), BF16),
            pltpu.VMEM((cb_n, 9, UPSCALE * UPSCALE, rb_n * BLOCK), F32),
            pltpu.VMEM((rb_n + 2, cb_n + 2, 8, BLOCK), F32),
            pltpu.SemaphoreType.DMA((4,)),
            pltpu.SemaphoreType.DMA((24,)),
            pltpu.SemaphoreType.DMA((24,)),
        ],
        compiler_params=pltpu.CompilerParams(collective_id=0, has_side_effects=True),
        name="flow",
    )(frame_one, frame_two, enc_weight, mask_weight)


def solution(mesh):
    in_specs = (P("lat", "lon", None), P("lat", "lon", None), P(), P())
    out_specs = P(None, "lat", "lon")
    return jax.shard_map(body, mesh=mesh, in_specs=in_specs, out_specs=out_specs, check_vma=False)
```

```python
import functools
import math

import jax
import jax.numpy as jnp
from jax import lax
from jax.experimental import pallas as pl
from jax.experimental.pallas import tpu as pltpu
from jax.sharding import PartitionSpec as P

BLOCK_ROWS = 8
BLOCK_COLS = 16
BLOCK = BLOCK_ROWS * BLOCK_COLS
UPSCALE = 8
F32 = jnp.float32
BF16 = jnp.bfloat16
MESH = pl.DeviceIdType.MESH


def iota(shape, axis):
    return lax.broadcasted_iota(jnp.int32, shape, axis)


def mm(a, b):
    return jnp.dot(a, b, preferred_element_type=F32)


def mm_nt(a, b):
    return lax.dot_general(a, b, (((1,), (1,)), ((), ())), preferred_element_type=F32)


def swap_groups(xs, lane_group):
    xs = list(xs)
    for bit in (1, 2, 4):
        mask = (lane_group & bit) != 0
        shift = bit * BLOCK_COLS
        for a in range(8):
            if a & bit:
                continue
            lo, hi = xs[a], xs[a | bit]
            xs[a] = jnp.where(mask, pltpu.roll(hi, shift, 1), lo)
            xs[a | bit] = jnp.where(mask, hi, pltpu.roll(lo, BLOCK - shift, 1))
    return xs


def kernel(
    f1, f2, w_hbm, mw_hbm, out,
    fr, wv, mv, wp, acc, hal, strip_s, strip_r, corner_s, corner_r, keys, qs, mix, fb,
    lsem, ssem, rsem,
):
    rows, cols, ch = f1.shape
    rb_n, cb_n = rows // BLOCK_ROWS, cols // BLOCK_COLS
    n_mask = mw_hbm.shape[0]
    lat, lon = lax.axis_index("lat"), lax.axis_index("lon")
    nlat, nlon = lax.axis_size("lat"), lax.axis_size("lon")
    has_n, has_s = lat > 0, lat < nlat - 1
    left = (lat, lax.rem(lon + nlon - 1, nlon))
    right = (lat, lax.rem(lon + 1, nlon))
    north, south = (lat - 1, lon), (lat + 1, lon)

    loads = [
        pltpu.make_async_copy(f1, fr.at[0, pl.ds(1, rows)], lsem.at[0]),
        pltpu.make_async_copy(f2, fr.at[1, pl.ds(1, rows)], lsem.at[1]),
        pltpu.make_async_copy(w_hbm, wv, lsem.at[2]),
        pltpu.make_async_copy(mw_hbm, mv, lsem.at[3]),
    ]
    for load in loads:
        load.start()

    barrier = pltpu.get_barrier_semaphore()

    def greet(peer):
        pl.semaphore_signal(barrier, inc=1, device_id=peer, device_id_type=MESH)

    greet(left)
    greet(right)
    pl.when(has_n)(lambda: greet(north))
    pl.when(has_s)(lambda: greet(south))

    def send(k, src, dst, peer):
        return pltpu.make_async_remote_copy(
            src_ref=src, dst_ref=dst, send_sem=ssem.at[k], recv_sem=rsem.at[k],
            device_id=peer, device_id_type=MESH,
        )

    zero_row = jnp.zeros((cols, ch), BF16)
    for f in range(2):
        fr[f, 0] = zero_row
        fr[f, rows + 1] = zero_row

    halo_rows = {
        0: [send(0, f1.at[0], hal.at[1, 0], north), send(1, f2.at[0], hal.at[1, 1], north)],
        1: [
            send(2, f1.at[rows - 1], hal.at[0, 0], south),
            send(3, f2.at[rows - 1], hal.at[0, 1], south),
        ],
    }
    strips = [
        send(4, strip_s.at[0], strip_r.at[1], left),
        send(5, strip_s.at[1], strip_r.at[0], right),
    ]
    corners = [
        send(6, corner_s.at[0], corner_r.at[1], left),
        send(7, corner_s.at[1], corner_r.at[0], right),
    ]

    def absent(side):
        return jnp.logical_not(has_n if side == 0 else has_s)

    def present(side):
        return has_n if side == 0 else has_s

    for side in range(2):

        @pl.when(absent(side))
        def _():
            hal[side] = jnp.zeros(hal.shape[1:], hal.dtype)
            lo = 0 if side == 0 else BLOCK_ROWS + rows
            keys[lo : lo + BLOCK_ROWS] = jnp.zeros((BLOCK_ROWS,) + keys.shape[1:], BF16)
            at = 0 if side == 0 else rb_n + 1
            fb[at] = jnp.zeros(fb.shape[1:], F32)

    loads[0].wait()
    loads[1].wait()
    for side in range(2):
        lo, pick = (0, 0) if side == 0 else (cols - 16, 15)
        for f in range(2):
            tile = fr[f, 1 : rows + 1, lo : lo + 16, :].astype(F32)
            one = jnp.sum(jnp.where(iota(tile.shape, 1) == pick, tile, 0.0), axis=1)
            strip_s[side, f * rows : (f + 1) * rows] = one.astype(BF16)

    pl.semaphore_wait(barrier, 2 + has_n.astype(jnp.int32) + has_s.astype(jnp.int32))

    for side in range(2):

        @pl.when(present(side))
        def _():
            for copy in halo_rows[side]:
                copy.start()

    for copy in strips:
        copy.start()

    loads[2].wait()

    def col_shift(y, side):
        flat = y.reshape(-1, ch)
        n = flat.shape[0]
        turned = pltpu.roll(flat, 1 if side == 0 else n - 1, 0).reshape(y.shape)
        edge = 0 if side == 0 else cols - 1
        return jnp.where(iota(y.shape, 1) == edge, 0.0, turned)

    for f in range(2):
        lhs = jnp.concatenate(
            [fr[f, a : a + rows].reshape(rows * cols, ch) for a in range(3)], axis=1
        )
        ys = [mm(lhs, wv[:, b].reshape(3 * ch, ch)).reshape(rows, cols, ch) for b in range(3)]
        acc[f] = ys[1] + col_shift(ys[0], 0) + col_shift(ys[2], 1)

    for side in range(2):

        @pl.when(present(side))
        def _():
            for copy in halo_rows[1 - side]:
                copy.wait_recv()

    for side in range(2):
        edge = 0 if side == 0 else cols - 1
        base = 0 if side == 0 else cols - 16
        got = jnp.zeros((16, ch), F32)
        for f in range(2):
            for end in range(2):
                tile = hal[end, f, base : base + 16, :].astype(F32)
                one = tile[edge - base : edge - base + 1]
                got = jnp.where(iota((16, ch), 0) == 2 * f + end, one, got)
        corner_s[side] = got.astype(BF16)
    for copy in corners:
        copy.start()

    for side in range(2):
        a = 0 if side == 0 else 2
        r = 0 if side == 0 else rows - 1
        flat = hal[side].reshape(2 * cols, ch)
        ys = [mm(flat, wv[a, b]).reshape(2, cols, ch) for b in range(3)]
        y = ys[1] + col_shift(ys[0], 0) + col_shift(ys[2], 1)
        for f in range(2):
            acc[f, r] = acc[f, r] + y[f]

    loads[3].wait()
    p = iota((n_mask, n_mask), 0)
    want = (p - (p & 63)) + ((p & 7) << 3) + ((p >> 3) & 7)
    perm = (iota((n_mask, n_mask), 1) == want).astype(F32).astype(BF16)
    wp[...] = mm(perm, mv[...]).astype(BF16)

    for copy in strips + corners:
        copy.wait_recv()
    row_id = iota((rows, ch), 0)
    rims = []
    for side in range(2):
        lhs = jnp.concatenate([strip_r[side], corner_r[side]], axis=0)
        rims.append([mm(lhs, wv[a, 2 * side]) for a in range(3)])

    def add_rim_columns(f):
        for side in range(2):
            z = rims[side]
            own = [z[a][f * rows : (f + 1) * rows] for a in range(3)]
            top = z[0][2 * rows + 2 * f : 2 * rows + 2 * f + 1]
            bottom = z[2][2 * rows + 2 * f + 1 : 2 * rows + 2 * f + 2]
            h = own[1] + jnp.where(row_id == 0, top, pltpu.roll(own[0], 1, 0))
            h = h + jnp.where(row_id == rows - 1, bottom, pltpu.roll(own[2], rows - 1, 0))
            lo, pick = (0, 0) if side == 0 else (cols - 8, 7)
            tile = acc[f, :, lo : lo + 8, :]
            acc[f, :, lo : lo + 8, :] = tile + jnp.where(
                iota(tile.shape, 1) == pick, h[:, None, :], 0.0
            )

    add_rim_columns(1)
    own_r = pl.ds(BLOCK_ROWS, rows)
    own_c = pl.ds(BLOCK_COLS, cols)
    keys[BLOCK_ROWS : BLOCK_ROWS + rows, BLOCK_COLS : BLOCK_COLS + cols] = acc[1].astype(BF16)

    br, bc = BLOCK_ROWS, BLOCK_COLS
    half = br // 2

    def rows_at(start, part):
        return pl.ds(start + part * half, half)

    key_rows = [
        [
            send(8 + part, keys.at[rows_at(br, part), own_c],
                 keys.at[rows_at(br + rows, part), own_c], north)
            for part in range(2)
        ],
        [
            send(26 + part, keys.at[rows_at(rows, part), own_c],
                 keys.at[rows_at(0, part), own_c], south)
            for part in range(2)
        ],
    ]
    first, last = pl.ds(bc, bc), pl.ds(cols, bc)
    to_left, to_right = pl.ds(bc + cols, bc), pl.ds(0, bc)
    key_cols = [
        send(10, keys.at[own_r, first], keys.at[own_r, to_left], left),
        send(11, keys.at[own_r, last], keys.at[own_r, to_right], right),
    ]
    key_corners = {}
    for side in range(2):
        key_corners[side] = []
        for part in range(2):
            r = rows_at(0 if side == 0 else br + rows, part)
            at = 12 + 2 * side + (0 if part == 0 else 16)
            key_corners[side] += [
                send(at, keys.at[r, first], keys.at[r, to_left], left),
                send(at + 1, keys.at[r, last], keys.at[r, to_right], right),
            ]
    for side in range(2):

        @pl.when(present(side))
        def _():
            for copy in key_rows[side]:
                copy.start()

    for copy in key_cols:
        copy.start()

    add_rim_columns(0)

    for cb in range(cb_n):
        for rb in range(rb_n):
            block = acc[0, rb * br : (rb + 1) * br, cb * bc : (cb + 1) * bc, :]
            qs[cb, rb * BLOCK : (rb + 1) * BLOCK] = block.astype(BF16).reshape(BLOCK, ch)

    scale = 1.0 / math.sqrt(ch)
    inside = [has_n.astype(F32), has_s.astype(F32)]
    zero = jnp.zeros((8, BLOCK), F32)
    totals = {(rb, cb): [zero, zero, zero] for rb in range(rb_n) for cb in range(cb_n)}
    sub = iota((8, BLOCK), 0).astype(F32)

    def correlate(kbs, kc):
        part = keys[kbs[0] * br : (kbs[-1] + 1) * br, kc * bc : (kc + 1) * bc, :]
        part = part.reshape(len(kbs) * BLOCK, ch)
        for cb in range(max(0, kc - 2), min(cb_n, kc + 1)):
            rbs = [rb for rb in range(rb_n) if any(0 <= kb - rb <= 2 for kb in kbs)]
            r0 = rbs[0]
            s = mm_nt(part, qs[cb, r0 * BLOCK : (rbs[-1] + 1) * BLOCK])
            for at, kb in enumerate(kbs):
                for rb in rbs:
                    if not 0 <= kb - rb <= 2:
                        continue
                    e = s[at * BLOCK : (at + 1) * BLOCK, (rb - r0) * BLOCK : (rb - r0 + 1) * BLOCK]
                    e = jnp.exp(e * scale).reshape(br, 2, 8, BLOCK)
                    lanes = [e[:, h] for h in range(2)]
                    by_row = lanes[0] + lanes[1]
                    y = by_row[0] * float(br * (kb - rb - 1))
                    for kr in range(1, br):
                        y = y + by_row[kr] * float(br * (kb - rb - 1) + kr)
                    by_col = [jnp.sum(h, axis=0) for h in lanes]
                    m = by_col[0] + by_col[1]
                    off = float(bc * (kc - cb - 1))
                    x = by_col[0] * (sub + off) + by_col[1] * (sub + (off + 8.0))
                    if kb == 0 or kb == rb_n + 1:
                        gate = inside[0] if kb == 0 else inside[1]
                        m, y, x = m * gate, y * gate, x * gate
                    old = totals[rb, cb]
                    totals[rb, cb] = [old[0] + m, old[1] + y, old[2] + x]

    own_kbs = list(range(1, rb_n + 1))
    for kc in range(1, cb_n + 1):
        correlate(own_kbs, kc)

    for cb in range(cb_n):
        logits = mm_nt(wp[...], qs[cb]).reshape(9, UPSCALE * UPSCALE, rb_n * BLOCK)
        e = jnp.exp(logits)
        mix[cb] = e / jnp.sum(e, axis=0, keepdims=True)

    def pass_on(side, part):
        @pl.when(present(side))
        def _():
            key_rows[1 - side][part].wait_recv()
            for copy in key_corners[side][2 * part : 2 * part + 2]:
                copy.start()

    for part in range(2):
        for side in range(2):
            pass_on(side, part)

    for kc in range(1, cb_n + 1):
        correlate([0], kc)
        correlate([rb_n + 1], kc)
    for copy in key_cols:
        copy.wait_recv()
    for kc in (0, cb_n + 1):
        correlate(own_kbs, kc)
    for side in range(2):

        @pl.when(present(side))
        def _():
            for copy in key_corners[side]:
                copy.wait_recv()

    for kc in (0, cb_n + 1):
        correlate([0], kc)
        correlate([rb_n + 1], kc)

    lane = iota((8, BLOCK), 1)
    sublane = iota((8, BLOCK), 0)
    qr, qc = lane >> 4, lane & 15
    for (rb, cb), (m, y, x) in totals.items():
        m, y, x = [jnp.sum(t, axis=0, keepdims=True) for t in (m, y, x)]
        fy = y / m - qr.astype(F32)
        fx = x / m - qc.astype(F32)
        both = jnp.where(sublane == 0, fy, fx) * float(UPSCALE)
        fb[rb + 1, cb + 1] = both

    flow_rows = [
        send(16, fb.at[1, pl.ds(1, cb_n)], fb.at[rb_n + 1, pl.ds(1, cb_n)], north),
        send(17, fb.at[rb_n, pl.ds(1, cb_n)], fb.at[0, pl.ds(1, cb_n)], south),
    ]
    flow_cols = [
        send(18, fb.at[pl.ds(1, rb_n), 1], fb.at[pl.ds(1, rb_n), cb_n + 1], left),
        send(19, fb.at[pl.ds(1, rb_n), cb_n], fb.at[pl.ds(1, rb_n), 0], right),
    ]
    flow_corners = {}
    for side in range(2):
        r = 0 if side == 0 else rb_n + 1
        flow_corners[side] = [
            send(20 + 2 * side, fb.at[r, 1], fb.at[r, cb_n + 1], left),
            send(21 + 2 * side, fb.at[r, cb_n], fb.at[r, 0], right),
        ]
    for side in range(2):

        @pl.when(present(side))
        def _():
            flow_rows[side].start()

    for copy in flow_cols:
        copy.start()
    for side in range(2):

        @pl.when(present(side))
        def _():
            flow_rows[1 - side].wait_recv()
            for copy in flow_corners[side]:
                copy.start()

    for copy in flow_cols:
        copy.wait_recv()
    for side in range(2):

        @pl.when(present(side))
        def _():
            for copy in flow_corners[side]:
                copy.wait_recv()

    k = iota((BLOCK, BLOCK), 0)
    weave = (iota((BLOCK, BLOCK), 1) == ((k & 15) << 3) + (k >> 4)).astype(F32).astype(BF16)

    for cb in range(cb_n):
        for rb in range(rb_n):
            shifted = {}
            for r in range(rb, rb + 3):
                mid = fb[r, cb + 1]
                shifted[r, 0] = jnp.where(
                    qc == 0, pltpu.roll(fb[r, cb], BLOCK - 15, 1), pltpu.roll(mid, 1, 1)
                )
                shifted[r, 1] = mid
                shifted[r, 2] = jnp.where(
                    qc == 15, pltpu.roll(fb[r, cb + 2], 15, 1), pltpu.roll(mid, BLOCK - 1, 1)
                )
            beside = []
            for a in range(3):
                for b in range(3):
                    here = shifted[rb + 1, b]
                    if a == 0:
                        here = pltpu.roll(jnp.where(qr == 7, shifted[rb, b], here), bc, 1)
                    if a == 2:
                        here = pltpu.roll(
                            jnp.where(qr == 0, shifted[rb + 2, b], here), BLOCK - bc, 1
                        )
                    beside.append(here)
            for d in range(2):
                up = jnp.zeros((UPSCALE * UPSCALE, BLOCK), F32)
                for n in range(9):
                    share = mix[cb, n, :, rb * BLOCK : (rb + 1) * BLOCK]
                    up = up + share * beside[n][d : d + 1]
                xs = [up[8 * j : 8 * j + 8] for j in range(8)]
                rowed = jnp.concatenate(swap_groups(xs, qr), axis=0)
                high = rowed.astype(BF16)
                rest = rowed - high.astype(F32)
                mid = rest.astype(BF16)
                low = (rest - mid.astype(F32)).astype(BF16)
                woven = mm(high, weave) + mm(mid, weave) + mm(low, weave)
                out[d, rb * 64 : (rb + 1) * 64, cb * BLOCK : (cb + 1) * BLOCK] = woven

    for side in range(2):

        @pl.when(present(side))
        def _():
            for copy in halo_rows[side] + key_rows[side] + [flow_rows[side]]:
                copy.wait_send()
            for copy in key_corners[side] + flow_corners[side]:
                copy.wait_send()

    for copy in strips + corners + key_cols + flow_cols:
        copy.wait_send()


def body(frame_one, frame_two, enc_weight, mask_weight):
    rows, cols, ch = frame_one.shape
    n_mask = mask_weight.shape[1]
    rb_n, cb_n = rows // BLOCK_ROWS, cols // BLOCK_COLS
    return pl.pallas_call(
        kernel,
        out_shape=jax.ShapeDtypeStruct((2, rows * UPSCALE, cols * UPSCALE), F32),
        in_specs=[pl.BlockSpec(memory_space=pl.ANY)] * 4,
        out_specs=pl.BlockSpec(memory_space=pltpu.VMEM),
        scratch_shapes=[
            pltpu.VMEM((2, rows + 2, cols, ch), BF16),
            pltpu.VMEM(enc_weight.shape, BF16),
            pltpu.VMEM((n_mask, ch), BF16),
            pltpu.VMEM((n_mask, ch), BF16),
            pltpu.VMEM((2, rows, cols, ch), F32),
            pltpu.VMEM((2, 2, cols, ch), BF16),
            pltpu.VMEM((2, 2 * rows, ch), BF16),
            pltpu.VMEM((2, 2 * rows, ch), BF16),
            pltpu.VMEM((2, 16, ch), BF16),
            pltpu.VMEM((2, 16, ch), BF16),
            pltpu.VMEM((rows + 2 * BLOCK_ROWS, cols + 2 * BLOCK_COLS, ch), BF16),
            pltpu.VMEM((cb_n, rb_n * BLOCK, ch), BF16),
            pltpu.VMEM((cb_n, 9, UPSCALE * UPSCALE, rb_n * BLOCK), F32),
            pltpu.VMEM((rb_n + 2, cb_n + 2, 8, BLOCK), F32),
            pltpu.SemaphoreType.DMA((4,)),
            pltpu.SemaphoreType.DMA((32,)),
            pltpu.SemaphoreType.DMA((32,)),
        ],
        compiler_params=pltpu.CompilerParams(collective_id=0, has_side_effects=True),
        name="flow",
    )(frame_one, frame_two, enc_weight, mask_weight.T)


def solution(mesh):
    in_specs = (P("lat", "lon", None), P("lat", "lon", None), P(), P())
    out_specs = P(None, "lat", "lon")
    return jax.shard_map(body, mesh=mesh, in_specs=in_specs, out_specs=out_specs, check_vma=False)
```

```python
import functools
import math

import jax
import jax.numpy as jnp
from jax import lax
from jax.experimental import pallas as pl
from jax.experimental.pallas import tpu as pltpu
from jax.sharding import PartitionSpec as P

BLOCK_ROWS = 8
BLOCK_COLS = 16
BLOCK = BLOCK_ROWS * BLOCK_COLS
UPSCALE = 8
F32 = jnp.float32
BF16 = jnp.bfloat16
MESH = pl.DeviceIdType.MESH


def iota(shape, axis):
    return lax.broadcasted_iota(jnp.int32, shape, axis)


def mm(a, b):
    return jnp.dot(a, b, preferred_element_type=F32)


def mm_nt(a, b):
    return lax.dot_general(a, b, (((1,), (1,)), ((), ())), preferred_element_type=F32)


def swap_groups(xs, lane_group):
    xs = list(xs)
    for bit in (1, 2, 4):
        mask = (lane_group & bit) != 0
        shift = bit * BLOCK_COLS
        for a in range(8):
            if a & bit:
                continue
            lo, hi = xs[a], xs[a | bit]
            xs[a] = jnp.where(mask, pltpu.roll(hi, shift, 1), lo)
            xs[a | bit] = jnp.where(mask, hi, pltpu.roll(lo, BLOCK - shift, 1))
    return xs


def kernel(
    f1, f2, w_hbm, mw_hbm, out,
    fr, wv, mv, wp, acc, hal, strip_s, strip_r, corner_s, corner_r, keys, qs, mix, fb,
    lsem, ssem, rsem,
):
    rows, cols, ch = f1.shape
    rb_n, cb_n = rows // BLOCK_ROWS, cols // BLOCK_COLS
    n_mask = mw_hbm.shape[0]
    lat, lon = lax.axis_index("lat"), lax.axis_index("lon")
    nlat, nlon = lax.axis_size("lat"), lax.axis_size("lon")
    has_n, has_s = lat > 0, lat < nlat - 1
    left = (lat, lax.rem(lon + nlon - 1, nlon))
    right = (lat, lax.rem(lon + 1, nlon))
    north, south = (lat - 1, lon), (lat + 1, lon)

    loads = [
        pltpu.make_async_copy(f1, fr.at[0, pl.ds(1, rows)], lsem.at[0]),
        pltpu.make_async_copy(f2, fr.at[1, pl.ds(1, rows)], lsem.at[1]),
        pltpu.make_async_copy(w_hbm, wv, lsem.at[2]),
        pltpu.make_async_copy(mw_hbm, mv, lsem.at[3]),
    ]
    for load in loads:
        load.start()

    barrier = pltpu.get_barrier_semaphore()

    def greet(peer):
        pl.semaphore_signal(barrier, inc=1, device_id=peer, device_id_type=MESH)

    greet(left)
    greet(right)
    pl.when(has_n)(lambda: greet(north))
    pl.when(has_s)(lambda: greet(south))

    def send(k, src, dst, peer):
        return pltpu.make_async_remote_copy(
            src_ref=src, dst_ref=dst, send_sem=ssem.at[k], recv_sem=rsem.at[k],
            device_id=peer, device_id_type=MESH,
        )

    zero_row = jnp.zeros((cols, ch), BF16)
    for f in range(2):
        fr[f, 0] = zero_row
        fr[f, rows + 1] = zero_row

    halo_rows = {
        0: [send(0, f1.at[0], hal.at[1, 0], north), send(1, f2.at[0], hal.at[1, 1], north)],
        1: [
            send(2, f1.at[rows - 1], hal.at[0, 0], south),
            send(3, f2.at[rows - 1], hal.at[0, 1], south),
        ],
    }
    strips = [
        send(4, strip_s.at[0], strip_r.at[1], left),
        send(5, strip_s.at[1], strip_r.at[0], right),
    ]
    corners = [
        send(6, corner_s.at[0], corner_r.at[1], left),
        send(7, corner_s.at[1], corner_r.at[0], right),
    ]

    def absent(side):
        return jnp.logical_not(has_n if side == 0 else has_s)

    def present(side):
        return has_n if side == 0 else has_s

    for side in range(2):

        @pl.when(absent(side))
        def _():
            hal[side] = jnp.zeros(hal.shape[1:], hal.dtype)
            lo = 0 if side == 0 else BLOCK_ROWS + rows
            keys[lo : lo + BLOCK_ROWS] = jnp.zeros((BLOCK_ROWS,) + keys.shape[1:], BF16)
            at = 0 if side == 0 else rb_n + 1
            fb[at] = jnp.zeros(fb.shape[1:], F32)

    loads[0].wait()
    loads[1].wait()
    for side in range(2):
        lo, pick = (0, 0) if side == 0 else (cols - 16, 15)
        for f in range(2):
            tile = fr[f, 1 : rows + 1, lo : lo + 16, :].astype(F32)
            one = jnp.sum(jnp.where(iota(tile.shape, 1) == pick, tile, 0.0), axis=1)
            strip_s[side, f * rows : (f + 1) * rows] = one.astype(BF16)

    pl.semaphore_wait(barrier, 2 + has_n.astype(jnp.int32) + has_s.astype(jnp.int32))

    for side in range(2):

        @pl.when(present(side))
        def _():
            for copy in halo_rows[side]:
                copy.start()

    for copy in strips:
        copy.start()

    loads[2].wait()

    def col_shift(y, side):
        flat = y.reshape(-1, ch)
        n = flat.shape[0]
        turned = pltpu.roll(flat, 1 if side == 0 else n - 1, 0).reshape(y.shape)
        edge = 0 if side == 0 else cols - 1
        return jnp.where(iota(y.shape, 1) == edge, 0.0, turned)

    for f in range(2):
        lhs = jnp.concatenate(
            [fr[f, a : a + rows].reshape(rows * cols, ch) for a in range(3)], axis=1
        )
        ys = [mm(lhs, wv[:, b].reshape(3 * ch, ch)).reshape(rows, cols, ch) for b in range(3)]
        acc[f] = ys[1] + col_shift(ys[0], 0) + col_shift(ys[2], 1)

    for side in range(2):

        @pl.when(present(side))
        def _():
            for copy in halo_rows[1 - side]:
                copy.wait_recv()

    for side in range(2):
        edge = 0 if side == 0 else cols - 1
        base = 0 if side == 0 else cols - 16
        got = jnp.zeros((16, ch), F32)
        for f in range(2):
            for end in range(2):
                tile = hal[end, f, base : base + 16, :].astype(F32)
                one = tile[edge - base : edge - base + 1]
                got = jnp.where(iota((16, ch), 0) == 2 * f + end, one, got)
        corner_s[side] = got.astype(BF16)
    for copy in corners:
        copy.start()

    for side in range(2):
        a = 0 if side == 0 else 2
        r = 0 if side == 0 else rows - 1
        flat = hal[side].reshape(2 * cols, ch)
        ys = [mm(flat, wv[a, b]).reshape(2, cols, ch) for b in range(3)]
        y = ys[1] + col_shift(ys[0], 0) + col_shift(ys[2], 1)
        for f in range(2):
            acc[f, r] = acc[f, r] + y[f]

    br, bc = BLOCK_ROWS, BLOCK_COLS
    own_r = pl.ds(br, rows)
    edge_w = 8
    mid = (bc + edge_w, cols - 2 * edge_w)
    lows, highs = (bc, edge_w), (bc + cols - edge_w, edge_w)

    def key_row_sends(k, span):
        c = pl.ds(*span)
        return [
            send(k, keys.at[pl.ds(br, br), c], keys.at[pl.ds(br + rows, br), c], north),
            send(k + 1, keys.at[pl.ds(rows, br), c], keys.at[pl.ds(0, br), c], south),
        ]

    def key_col_sends(k, r, early):
        off = edge_w if early else 0
        back = 0 if early else edge_w
        return [
            send(k, keys.at[r, pl.ds(bc + off, edge_w)],
                 keys.at[r, pl.ds(bc + cols + off, edge_w)], left),
            send(k + 1, keys.at[r, pl.ds(cols + back, edge_w)],
                 keys.at[r, pl.ds(back, edge_w)], right),
        ]

    rows_mid = key_row_sends(8, mid)
    rows_low = key_row_sends(10, lows)
    rows_high = key_row_sends(12, highs)
    cols_early = key_col_sends(14, own_r, True)
    cols_late = key_col_sends(24, own_r, False)
    corners_early, corners_late = {}, {}
    for side in range(2):
        r = pl.ds(0 if side == 0 else br + rows, br)
        corners_early[side] = key_col_sends(26 + 4 * side, r, True)
        corners_late[side] = key_col_sends(28 + 4 * side, r, False)

    keys[br : br + rows, mid[0] : mid[0] + mid[1]] = acc[
        1, :, edge_w : cols - edge_w, :
    ].astype(BF16)
    for side in range(2):

        @pl.when(present(side))
        def _():
            rows_mid[side].start()

    for copy in cols_early:
        copy.start()

    loads[3].wait()
    p = iota((n_mask, n_mask), 0)
    want = (p - (p & 63)) + ((p & 7) << 3) + ((p >> 3) & 7)
    perm = (iota((n_mask, n_mask), 1) == want).astype(F32).astype(BF16)
    wp[...] = mm(perm, mv[...]).astype(BF16)

    for copy in strips + corners:
        copy.wait_recv()
    row_id = iota((rows, ch), 0)
    rims = []
    for side in range(2):
        lhs = jnp.concatenate([strip_r[side], corner_r[side]], axis=0)
        rims.append([mm(lhs, wv[a, 2 * side]) for a in range(3)])

    def add_rim_columns(f):
        for side in range(2):
            z = rims[side]
            own = [z[a][f * rows : (f + 1) * rows] for a in range(3)]
            top = z[0][2 * rows + 2 * f : 2 * rows + 2 * f + 1]
            bottom = z[2][2 * rows + 2 * f + 1 : 2 * rows + 2 * f + 2]
            h = own[1] + jnp.where(row_id == 0, top, pltpu.roll(own[0], 1, 0))
            h = h + jnp.where(row_id == rows - 1, bottom, pltpu.roll(own[2], rows - 1, 0))
            lo, pick = (0, 0) if side == 0 else (cols - 8, 7)
            tile = acc[f, :, lo : lo + 8, :]
            acc[f, :, lo : lo + 8, :] = tile + jnp.where(
                iota(tile.shape, 1) == pick, h[:, None, :], 0.0
            )

    add_rim_columns(1)
    for lo in (0, cols - edge_w):
        keys[br : br + rows, bc + lo : bc + lo + edge_w] = acc[
            1, :, lo : lo + edge_w, :
        ].astype(BF16)
    for side in range(2):

        @pl.when(present(side))
        def _():
            rows_low[side].start()
            rows_high[side].start()

    for copy in cols_late:
        copy.start()

    add_rim_columns(0)

    for cb in range(cb_n):
        for rb in range(rb_n):
            block = acc[0, rb * br : (rb + 1) * br, cb * bc : (cb + 1) * bc, :]
            qs[cb, rb * BLOCK : (rb + 1) * BLOCK] = block.astype(BF16).reshape(BLOCK, ch)

    scale = 1.0 / math.sqrt(ch)
    inside = [has_n.astype(F32), has_s.astype(F32)]
    zero = jnp.zeros((8, BLOCK), F32)
    totals = {(rb, cb): [zero, zero, zero] for rb in range(rb_n) for cb in range(cb_n)}
    sub = iota((8, BLOCK), 0).astype(F32)

    def correlate(kbs, kc):
        part = keys[kbs[0] * br : (kbs[-1] + 1) * br, kc * bc : (kc + 1) * bc, :]
        part = part.reshape(len(kbs) * BLOCK, ch)
        for cb in range(max(0, kc - 2), min(cb_n, kc + 1)):
            rbs = [rb for rb in range(rb_n) if any(0 <= kb - rb <= 2 for kb in kbs)]
            r0 = rbs[0]
            s = mm_nt(part, qs[cb, r0 * BLOCK : (rbs[-1] + 1) * BLOCK])
            for at, kb in enumerate(kbs):
                for rb in rbs:
                    if not 0 <= kb - rb <= 2:
                        continue
                    e = s[at * BLOCK : (at + 1) * BLOCK, (rb - r0) * BLOCK : (rb - r0 + 1) * BLOCK]
                    e = jnp.exp(e * scale).reshape(br, 2, 8, BLOCK)
                    lanes = [e[:, h] for h in range(2)]
                    by_row = lanes[0] + lanes[1]
                    y = by_row[0] * float(br * (kb - rb - 1))
                    for kr in range(1, br):
                        y = y + by_row[kr] * float(br * (kb - rb - 1) + kr)
                    by_col = [jnp.sum(h, axis=0) for h in lanes]
                    m = by_col[0] + by_col[1]
                    off = float(bc * (kc - cb - 1))
                    x = by_col[0] * (sub + off) + by_col[1] * (sub + (off + 8.0))
                    if kb == 0 or kb == rb_n + 1:
                        gate = inside[0] if kb == 0 else inside[1]
                        m, y, x = m * gate, y * gate, x * gate
                    old = totals[rb, cb]
                    totals[rb, cb] = [old[0] + m, old[1] + y, old[2] + x]

    own_kbs = list(range(1, rb_n + 1))
    for kc in range(1, cb_n + 1):
        correlate(own_kbs, kc)

    def pass_on(arrivals, relays):
        for side in range(2):

            @pl.when(present(side))
            def _():
                for rows_sent in arrivals:
                    rows_sent[1 - side].wait_recv()
                for copy in relays[side]:
                    copy.start()

    pass_on([rows_mid], corners_early)

    for cb in range(cb_n):
        logits = mm_nt(wp[...], qs[cb]).reshape(9, UPSCALE * UPSCALE, rb_n * BLOCK)
        e = jnp.exp(logits)
        mix[cb] = e / jnp.sum(e, axis=0, keepdims=True)

    pass_on([rows_low, rows_high], corners_late)

    for kc in range(1, cb_n + 1):
        correlate([0], kc)
        correlate([rb_n + 1], kc)
    for copy in cols_early + cols_late:
        copy.wait_recv()
    for kc in (0, cb_n + 1):
        correlate(own_kbs, kc)
    for side in range(2):

        @pl.when(present(side))
        def _():
            for copy in corners_early[side] + corners_late[side]:
                copy.wait_recv()

    for kc in (0, cb_n + 1):
        correlate([0], kc)
        correlate([rb_n + 1], kc)

    lane = iota((8, BLOCK), 1)
    sublane = iota((8, BLOCK), 0)
    qr, qc = lane >> 4, lane & 15
    for (rb, cb), (m, y, x) in totals.items():
        m, y, x = [jnp.sum(t, axis=0, keepdims=True) for t in (m, y, x)]
        fy = y / m - qr.astype(F32)
        fx = x / m - qc.astype(F32)
        both = jnp.where(sublane == 0, fy, fx) * float(UPSCALE)
        fb[rb + 1, cb + 1] = both

    flow_rows = [
        send(16, fb.at[1, pl.ds(1, cb_n)], fb.at[rb_n + 1, pl.ds(1, cb_n)], north),
        send(17, fb.at[rb_n, pl.ds(1, cb_n)], fb.at[0, pl.ds(1, cb_n)], south),
    ]
    flow_cols = [
        send(18, fb.at[pl.ds(1, rb_n), 1], fb.at[pl.ds(1, rb_n), cb_n + 1], left),
        send(19, fb.at[pl.ds(1, rb_n), cb_n], fb.at[pl.ds(1, rb_n), 0], right),
    ]
    flow_corners = {}
    for side in range(2):
        r = 0 if side == 0 else rb_n + 1
        flow_corners[side] = [
            send(20 + 2 * side, fb.at[r, 1], fb.at[r, cb_n + 1], left),
            send(21 + 2 * side, fb.at[r, cb_n], fb.at[r, 0], right),
        ]
    for side in range(2):

        @pl.when(present(side))
        def _():
            flow_rows[side].start()

    for copy in flow_cols:
        copy.start()
    for side in range(2):

        @pl.when(present(side))
        def _():
            flow_rows[1 - side].wait_recv()
            for copy in flow_corners[side]:
                copy.start()

    for copy in flow_cols:
        copy.wait_recv()
    for side in range(2):

        @pl.when(present(side))
        def _():
            for copy in flow_corners[side]:
                copy.wait_recv()

    k = iota((BLOCK, BLOCK), 0)
    weave = (iota((BLOCK, BLOCK), 1) == ((k & 15) << 3) + (k >> 4)).astype(F32).astype(BF16)

    for cb in range(cb_n):
        for rb in range(rb_n):
            shifted = {}
            for r in range(rb, rb + 3):
                mid = fb[r, cb + 1]
                shifted[r, 0] = jnp.where(
                    qc == 0, pltpu.roll(fb[r, cb], BLOCK - 15, 1), pltpu.roll(mid, 1, 1)
                )
                shifted[r, 1] = mid
                shifted[r, 2] = jnp.where(
                    qc == 15, pltpu.roll(fb[r, cb + 2], 15, 1), pltpu.roll(mid, BLOCK - 1, 1)
                )
            beside = []
            for a in range(3):
                for b in range(3):
                    here = shifted[rb + 1, b]
                    if a == 0:
                        here = pltpu.roll(jnp.where(qr == 7, shifted[rb, b], here), bc, 1)
                    if a == 2:
                        here = pltpu.roll(
                            jnp.where(qr == 0, shifted[rb + 2, b], here), BLOCK - bc, 1
                        )
                    beside.append(here)
            for d in range(2):
                up = jnp.zeros((UPSCALE * UPSCALE, BLOCK), F32)
                for n in range(9):
                    share = mix[cb, n, :, rb * BLOCK : (rb + 1) * BLOCK]
                    up = up + share * beside[n][d : d + 1]
                xs = [up[8 * j : 8 * j + 8] for j in range(8)]
                rowed = jnp.concatenate(swap_groups(xs, qr), axis=0)
                high = rowed.astype(BF16)
                rest = rowed - high.astype(F32)
                mid = rest.astype(BF16)
                low = (rest - mid.astype(F32)).astype(BF16)
                woven = mm(high, weave) + mm(mid, weave) + mm(low, weave)
                out[d, rb * 64 : (rb + 1) * 64, cb * BLOCK : (cb + 1) * BLOCK] = woven

    for side in range(2):

        @pl.when(present(side))
        def _():
            for copy in halo_rows[side] + [
                rows_mid[side], rows_low[side], rows_high[side], flow_rows[side]
            ]:
                copy.wait_send()
            for copy in corners_early[side] + corners_late[side] + flow_corners[side]:
                copy.wait_send()

    for copy in strips + corners + cols_early + cols_late + flow_cols:
        copy.wait_send()


def body(frame_one, frame_two, enc_weight, mask_weight):
    rows, cols, ch = frame_one.shape
    n_mask = mask_weight.shape[1]
    rb_n, cb_n = rows // BLOCK_ROWS, cols // BLOCK_COLS
    return pl.pallas_call(
        kernel,
        out_shape=jax.ShapeDtypeStruct((2, rows * UPSCALE, cols * UPSCALE), F32),
        in_specs=[pl.BlockSpec(memory_space=pl.ANY)] * 4,
        out_specs=pl.BlockSpec(memory_space=pltpu.VMEM),
        scratch_shapes=[
            pltpu.VMEM((2, rows + 2, cols, ch), BF16),
            pltpu.VMEM(enc_weight.shape, BF16),
            pltpu.VMEM((n_mask, ch), BF16),
            pltpu.VMEM((n_mask, ch), BF16),
            pltpu.VMEM((2, rows, cols, ch), F32),
            pltpu.VMEM((2, 2, cols, ch), BF16),
            pltpu.VMEM((2, 2 * rows, ch), BF16),
            pltpu.VMEM((2, 2 * rows, ch), BF16),
            pltpu.VMEM((2, 16, ch), BF16),
            pltpu.VMEM((2, 16, ch), BF16),
            pltpu.VMEM((rows + 2 * BLOCK_ROWS, cols + 2 * BLOCK_COLS, ch), BF16),
            pltpu.VMEM((cb_n, rb_n * BLOCK, ch), BF16),
            pltpu.VMEM((cb_n, 9, UPSCALE * UPSCALE, rb_n * BLOCK), F32),
            pltpu.VMEM((rb_n + 2, cb_n + 2, 8, BLOCK), F32),
            pltpu.SemaphoreType.DMA((4,)),
            pltpu.SemaphoreType.DMA((34,)),
            pltpu.SemaphoreType.DMA((34,)),
        ],
        compiler_params=pltpu.CompilerParams(collective_id=0, has_side_effects=True),
        name="flow",
    )(frame_one, frame_two, enc_weight, mask_weight.T)


def solution(mesh):
    in_specs = (P("lat", "lon", None), P("lat", "lon", None), P(), P())
    out_specs = P(None, "lat", "lon")
    return jax.shard_map(body, mesh=mesh, in_specs=in_specs, out_specs=out_specs, check_vma=False)
```

```python
import functools
import math

import jax
import jax.numpy as jnp
from jax import lax
from jax.experimental import pallas as pl
from jax.experimental.pallas import tpu as pltpu
from jax.sharding import PartitionSpec as P

BLOCK_ROWS = 8
BLOCK_COLS = 16
BLOCK = BLOCK_ROWS * BLOCK_COLS
UPSCALE = 8
F32 = jnp.float32
BF16 = jnp.bfloat16
MESH = pl.DeviceIdType.MESH


def iota(shape, axis):
    return lax.broadcasted_iota(jnp.int32, shape, axis)


def mm(a, b):
    return jnp.dot(a, b, preferred_element_type=F32)


def mm_nt(a, b):
    return lax.dot_general(a, b, (((1,), (1,)), ((), ())), preferred_element_type=F32)


def swap_groups(xs, lane_group):
    xs = list(xs)
    for bit in (1, 2, 4):
        mask = (lane_group & bit) != 0
        shift = bit * BLOCK_COLS
        for a in range(8):
            if a & bit:
                continue
            lo, hi = xs[a], xs[a | bit]
            xs[a] = jnp.where(mask, pltpu.roll(hi, shift, 1), lo)
            xs[a | bit] = jnp.where(mask, hi, pltpu.roll(lo, BLOCK - shift, 1))
    return xs


def kernel(
    f1, f2, w_hbm, mw_hbm, out,
    fr, wv, mv, wp, acc, hal, strip_s, strip_r, corner_s, corner_r, keys, qs, mix, fb,
    lsem, ssem, rsem,
):
    rows, cols, ch = f1.shape
    rb_n, cb_n = rows // BLOCK_ROWS, cols // BLOCK_COLS
    n_mask = mw_hbm.shape[0]
    lat, lon = lax.axis_index("lat"), lax.axis_index("lon")
    nlat, nlon = lax.axis_size("lat"), lax.axis_size("lon")
    has_n, has_s = lat > 0, lat < nlat - 1
    left = (lat, lax.rem(lon + nlon - 1, nlon))
    right = (lat, lax.rem(lon + 1, nlon))
    north, south = (lat - 1, lon), (lat + 1, lon)

    loads = [
        pltpu.make_async_copy(f1, fr.at[0, pl.ds(1, rows)], lsem.at[0]),
        pltpu.make_async_copy(f2, fr.at[1, pl.ds(1, rows)], lsem.at[1]),
        pltpu.make_async_copy(w_hbm, wv, lsem.at[2]),
        pltpu.make_async_copy(mw_hbm, mv, lsem.at[3]),
    ]
    for load in loads:
        load.start()

    barrier = pltpu.get_barrier_semaphore()

    def greet(peer):
        pl.semaphore_signal(barrier, inc=1, device_id=peer, device_id_type=MESH)

    greet(left)
    greet(right)
    pl.when(has_n)(lambda: greet(north))
    pl.when(has_s)(lambda: greet(south))

    def send(k, src, dst, peer):
        return pltpu.make_async_remote_copy(
            src_ref=src, dst_ref=dst, send_sem=ssem.at[k], recv_sem=rsem.at[k],
            device_id=peer, device_id_type=MESH,
        )

    zero_row = jnp.zeros((cols, ch), BF16)
    for f in range(2):
        fr[f, 0] = zero_row
        fr[f, rows + 1] = zero_row

    halo_rows = {
        0: [send(0, f1.at[0], hal.at[1, 0], north), send(1, f2.at[0], hal.at[1, 1], north)],
        1: [
            send(2, f1.at[rows - 1], hal.at[0, 0], south),
            send(3, f2.at[rows - 1], hal.at[0, 1], south),
        ],
    }
    strips = [
        send(4, strip_s.at[0], strip_r.at[1], left),
        send(5, strip_s.at[1], strip_r.at[0], right),
    ]
    corners = [
        send(6, corner_s.at[0], corner_r.at[1], left),
        send(7, corner_s.at[1], corner_r.at[0], right),
    ]

    def absent(side):
        return jnp.logical_not(has_n if side == 0 else has_s)

    def present(side):
        return has_n if side == 0 else has_s

    for side in range(2):

        @pl.when(absent(side))
        def _():
            hal[side] = jnp.zeros(hal.shape[1:], hal.dtype)
            lo = 0 if side == 0 else BLOCK_ROWS + rows
            keys[lo : lo + BLOCK_ROWS] = jnp.zeros((BLOCK_ROWS,) + keys.shape[1:], BF16)
            at = 0 if side == 0 else rb_n + 1
            fb[at] = jnp.zeros(fb.shape[1:], F32)

    loads[0].wait()
    loads[1].wait()
    for side in range(2):
        lo, pick = (0, 0) if side == 0 else (cols - 16, 15)
        for f in range(2):
            tile = fr[f, 1 : rows + 1, lo : lo + 16, :].astype(F32)
            one = jnp.sum(jnp.where(iota(tile.shape, 1) == pick, tile, 0.0), axis=1)
            strip_s[side, f * rows : (f + 1) * rows] = one.astype(BF16)

    pl.semaphore_wait(barrier, 2 + has_n.astype(jnp.int32) + has_s.astype(jnp.int32))

    for side in range(2):

        @pl.when(present(side))
        def _():
            for copy in halo_rows[side]:
                copy.start()

    for copy in strips:
        copy.start()

    loads[2].wait()

    def col_shift(y, side):
        flat = y.reshape(-1, ch)
        n = flat.shape[0]
        turned = pltpu.roll(flat, 1 if side == 0 else n - 1, 0).reshape(y.shape)
        edge = 0 if side == 0 else cols - 1
        return jnp.where(iota(y.shape, 1) == edge, 0.0, turned)

    for f in range(2):
        lhs = jnp.concatenate(
            [fr[f, a : a + rows].reshape(rows * cols, ch) for a in range(3)], axis=1
        )
        ys = [mm(lhs, wv[:, b].reshape(3 * ch, ch)).reshape(rows, cols, ch) for b in range(3)]
        acc[f] = ys[1] + col_shift(ys[0], 0) + col_shift(ys[2], 1)

    for side in range(2):

        @pl.when(present(side))
        def _():
            for copy in halo_rows[1 - side]:
                copy.wait_recv()

    for side in range(2):
        edge = 0 if side == 0 else cols - 1
        base = 0 if side == 0 else cols - 16
        got = jnp.zeros((16, ch), F32)
        for f in range(2):
            for end in range(2):
                tile = hal[end, f, base : base + 16, :].astype(F32)
                one = tile[edge - base : edge - base + 1]
                got = jnp.where(iota((16, ch), 0) == 2 * f + end, one, got)
        corner_s[side] = got.astype(BF16)
    for copy in corners:
        copy.start()

    for side in range(2):
        a = 0 if side == 0 else 2
        r = 0 if side == 0 else rows - 1
        flat = hal[side].reshape(2 * cols, ch)
        ys = [mm(flat, wv[a, b]).reshape(2, cols, ch) for b in range(3)]
        y = ys[1] + col_shift(ys[0], 0) + col_shift(ys[2], 1)
        for f in range(2):
            acc[f, r] = acc[f, r] + y[f]

    br, bc = BLOCK_ROWS, BLOCK_COLS
    own_r = pl.ds(br, rows)
    edge_w = 8
    mid = (bc + edge_w, cols - 2 * edge_w)
    lows, highs = (bc, edge_w), (bc + cols - edge_w, edge_w)

    def key_row_sends(k, span):
        c = pl.ds(*span)
        return [
            send(k, keys.at[pl.ds(br, br), c], keys.at[pl.ds(br + rows, br), c], north),
            send(k + 1, keys.at[pl.ds(rows, br), c], keys.at[pl.ds(0, br), c], south),
        ]

    def key_col_sends(k, r, early):
        off = edge_w if early else 0
        back = 0 if early else edge_w
        return [
            send(k, keys.at[r, pl.ds(bc + off, edge_w)],
                 keys.at[r, pl.ds(bc + cols + off, edge_w)], left),
            send(k + 1, keys.at[r, pl.ds(cols + back, edge_w)],
                 keys.at[r, pl.ds(back, edge_w)], right),
        ]

    rows_mid = key_row_sends(8, mid)
    rows_low = key_row_sends(10, lows)
    rows_high = key_row_sends(12, highs)
    cols_early = key_col_sends(14, own_r, True)
    cols_late = key_col_sends(24, own_r, False)
    corners_early, corners_late = {}, {}
    for side in range(2):
        r = pl.ds(0 if side == 0 else br + rows, br)
        corners_early[side] = key_col_sends(26 + 4 * side, r, True)
        corners_late[side] = key_col_sends(28 + 4 * side, r, False)

    keys[br : br + rows, mid[0] : mid[0] + mid[1]] = acc[
        1, :, edge_w : cols - edge_w, :
    ].astype(BF16)
    for side in range(2):

        @pl.when(present(side))
        def _():
            rows_mid[side].start()

    for copy in cols_early:
        copy.start()

    loads[3].wait()
    p = iota((n_mask, n_mask), 0)
    want = (p - (p & 63)) + ((p & 7) << 3) + ((p >> 3) & 7)
    perm = (iota((n_mask, n_mask), 1) == want).astype(F32).astype(BF16)
    wp[...] = mm(perm, mv[...]).astype(BF16)

    for copy in strips + corners:
        copy.wait_recv()
    row_id = iota((rows, ch), 0)
    rims = []
    for side in range(2):
        lhs = jnp.concatenate([strip_r[side], corner_r[side]], axis=0)
        rims.append([mm(lhs, wv[a, 2 * side]) for a in range(3)])

    def add_rim_columns(f):
        for side in range(2):
            z = rims[side]
            own = [z[a][f * rows : (f + 1) * rows] for a in range(3)]
            top = z[0][2 * rows + 2 * f : 2 * rows + 2 * f + 1]
            bottom = z[2][2 * rows + 2 * f + 1 : 2 * rows + 2 * f + 2]
            h = own[1] + jnp.where(row_id == 0, top, pltpu.roll(own[0], 1, 0))
            h = h + jnp.where(row_id == rows - 1, bottom, pltpu.roll(own[2], rows - 1, 0))
            lo, pick = (0, 0) if side == 0 else (cols - 8, 7)
            tile = acc[f, :, lo : lo + 8, :]
            acc[f, :, lo : lo + 8, :] = tile + jnp.where(
                iota(tile.shape, 1) == pick, h[:, None, :], 0.0
            )

    add_rim_columns(1)
    for lo in (0, cols - edge_w):
        keys[br : br + rows, bc + lo : bc + lo + edge_w] = acc[
            1, :, lo : lo + edge_w, :
        ].astype(BF16)
    for side in range(2):

        @pl.when(present(side))
        def _():
            rows_low[side].start()
            rows_high[side].start()

    for copy in cols_late:
        copy.start()

    add_rim_columns(0)

    for cb in range(cb_n):
        for rb in range(rb_n):
            block = acc[0, rb * br : (rb + 1) * br, cb * bc : (cb + 1) * bc, :]
            qs[cb, rb * BLOCK : (rb + 1) * BLOCK] = block.astype(BF16).reshape(BLOCK, ch)

    scale = 1.0 / math.sqrt(ch)
    inside = [has_n.astype(F32), has_s.astype(F32)]
    zero = jnp.zeros((8, BLOCK), F32)
    totals = {(rb, cb): [zero, zero, zero] for rb in range(rb_n) for cb in range(cb_n)}
    sub = iota((8, BLOCK), 0).astype(F32)

    def correlate(kbs, kc):
        part = keys[kbs[0] * br : (kbs[-1] + 1) * br, kc * bc : (kc + 1) * bc, :]
        part = part.reshape(len(kbs) * BLOCK, ch)
        for cb in range(max(0, kc - 2), min(cb_n, kc + 1)):
            rbs = [rb for rb in range(rb_n) if any(0 <= kb - rb <= 2 for kb in kbs)]
            r0 = rbs[0]
            s = mm_nt(part, qs[cb, r0 * BLOCK : (rbs[-1] + 1) * BLOCK])
            for at, kb in enumerate(kbs):
                for rb in rbs:
                    if not 0 <= kb - rb <= 2:
                        continue
                    e = s[at * BLOCK : (at + 1) * BLOCK, (rb - r0) * BLOCK : (rb - r0 + 1) * BLOCK]
                    e = jnp.exp(e * scale).reshape(br, 2, 8, BLOCK)
                    lanes = [e[:, h] for h in range(2)]
                    by_row = lanes[0] + lanes[1]
                    y = by_row[0] * float(br * (kb - rb - 1))
                    for kr in range(1, br):
                        y = y + by_row[kr] * float(br * (kb - rb - 1) + kr)
                    by_col = [jnp.sum(h, axis=0) for h in lanes]
                    m = by_col[0] + by_col[1]
                    off = float(bc * (kc - cb - 1))
                    x = by_col[0] * (sub + off) + by_col[1] * (sub + (off + 8.0))
                    if kb == 0 or kb == rb_n + 1:
                        gate = inside[0] if kb == 0 else inside[1]
                        m, y, x = m * gate, y * gate, x * gate
                    old = totals[rb, cb]
                    totals[rb, cb] = [old[0] + m, old[1] + y, old[2] + x]

    own_kbs = list(range(1, rb_n + 1))
    for kc in range(1, cb_n + 1):
        correlate(own_kbs, kc)

    def pass_on(arrivals, relays):
        for side in range(2):

            @pl.when(present(side))
            def _():
                for rows_sent in arrivals:
                    rows_sent[1 - side].wait_recv()
                for copy in relays[side]:
                    copy.start()

    pass_on([rows_mid], corners_early)

    for cb in range(cb_n):
        logits = mm_nt(wp[...], qs[cb]).reshape(9, UPSCALE * UPSCALE, rb_n * BLOCK)
        e = jnp.exp(logits)
        mix[cb] = e / jnp.sum(e, axis=0, keepdims=True)

    pass_on([rows_low, rows_high], corners_late)

    for kc in range(1, cb_n + 1):
        correlate([0], kc)
        correlate([rb_n + 1], kc)
    for copy in cols_early + cols_late:
        copy.wait_recv()
    for kc in (0, cb_n + 1):
        correlate(own_kbs, kc)
    for side in range(2):

        @pl.when(present(side))
        def _():
            for copy in corners_early[side] + corners_late[side]:
                copy.wait_recv()

    for kc in (0, cb_n + 1):
        correlate([0], kc)
        correlate([rb_n + 1], kc)

    lane = iota((8, BLOCK), 1)
    sublane = iota((8, BLOCK), 0)
    qr, qc = lane >> 4, lane & 15
    for (rb, cb), (m, y, x) in totals.items():
        m, y, x = [jnp.sum(t, axis=0, keepdims=True) for t in (m, y, x)]
        fy = y / m - qr.astype(F32)
        fx = x / m - qc.astype(F32)
        both = jnp.where(sublane == 0, fy, fx) * float(UPSCALE)
        fb[rb + 1, cb + 1] = both

    flow_rows = [
        send(16, fb.at[1, pl.ds(1, cb_n)], fb.at[rb_n + 1, pl.ds(1, cb_n)], north),
        send(17, fb.at[rb_n, pl.ds(1, cb_n)], fb.at[0, pl.ds(1, cb_n)], south),
    ]
    flow_cols = [
        send(18, fb.at[pl.ds(1, rb_n), 1], fb.at[pl.ds(1, rb_n), cb_n + 1], left),
        send(19, fb.at[pl.ds(1, rb_n), cb_n], fb.at[pl.ds(1, rb_n), 0], right),
    ]
    flow_corners = {}
    for side in range(2):
        src_r, dst_r = (1, rb_n + 1) if side == 0 else (rb_n, 0)
        to = lat - 1 if side == 0 else lat + 1
        flow_corners[side] = [
            send(20 + 2 * side, fb.at[src_r, 1], fb.at[dst_r, cb_n + 1], (to, left[1])),
            send(21 + 2 * side, fb.at[src_r, cb_n], fb.at[dst_r, 0], (to, right[1])),
        ]
    for side in range(2):

        @pl.when(present(side))
        def _():
            for copy in flow_corners[side] + [flow_rows[side]]:
                copy.start()

    for copy in flow_cols:
        copy.start()
    for copy in flow_cols:
        copy.wait_recv()
    for side in range(2):

        @pl.when(present(side))
        def _():
            for copy in flow_corners[1 - side] + [flow_rows[1 - side]]:
                copy.wait_recv()

    k = iota((BLOCK, BLOCK), 0)
    weave = (iota((BLOCK, BLOCK), 1) == ((k & 15) << 3) + (k >> 4)).astype(F32).astype(BF16)

    for cb in range(cb_n):
        for rb in range(rb_n):
            shifted = {}
            for r in range(rb, rb + 3):
                mid = fb[r, cb + 1]
                shifted[r, 0] = jnp.where(
                    qc == 0, pltpu.roll(fb[r, cb], BLOCK - 15, 1), pltpu.roll(mid, 1, 1)
                )
                shifted[r, 1] = mid
                shifted[r, 2] = jnp.where(
                    qc == 15, pltpu.roll(fb[r, cb + 2], 15, 1), pltpu.roll(mid, BLOCK - 1, 1)
                )
            beside = []
            for a in range(3):
                for b in range(3):
                    here = shifted[rb + 1, b]
                    if a == 0:
                        here = pltpu.roll(jnp.where(qr == 7, shifted[rb, b], here), bc, 1)
                    if a == 2:
                        here = pltpu.roll(
                            jnp.where(qr == 0, shifted[rb + 2, b], here), BLOCK - bc, 1
                        )
                    beside.append(here)
            for d in range(2):
                up = jnp.zeros((UPSCALE * UPSCALE, BLOCK), F32)
                for n in range(9):
                    share = mix[cb, n, :, rb * BLOCK : (rb + 1) * BLOCK]
                    up = up + share * beside[n][d : d + 1]
                xs = [up[8 * j : 8 * j + 8] for j in range(8)]
                rowed = jnp.concatenate(swap_groups(xs, qr), axis=0)
                high = rowed.astype(BF16)
                rest = rowed - high.astype(F32)
                mid = rest.astype(BF16)
                low = (rest - mid.astype(F32)).astype(BF16)
                woven = mm(high, weave) + mm(mid, weave) + mm(low, weave)
                out[d, rb * 64 : (rb + 1) * 64, cb * BLOCK : (cb + 1) * BLOCK] = woven

    for side in range(2):

        @pl.when(present(side))
        def _():
            for copy in halo_rows[side] + [
                rows_mid[side], rows_low[side], rows_high[side], flow_rows[side]
            ]:
                copy.wait_send()
            for copy in corners_early[side] + corners_late[side] + flow_corners[side]:
                copy.wait_send()

    for copy in strips + corners + cols_early + cols_late + flow_cols:
        copy.wait_send()


def body(frame_one, frame_two, enc_weight, mask_weight):
    rows, cols, ch = frame_one.shape
    n_mask = mask_weight.shape[1]
    rb_n, cb_n = rows // BLOCK_ROWS, cols // BLOCK_COLS
    return pl.pallas_call(
        kernel,
        out_shape=jax.ShapeDtypeStruct((2, rows * UPSCALE, cols * UPSCALE), F32),
        in_specs=[pl.BlockSpec(memory_space=pl.ANY)] * 4,
        out_specs=pl.BlockSpec(memory_space=pltpu.VMEM),
        scratch_shapes=[
            pltpu.VMEM((2, rows + 2, cols, ch), BF16),
            pltpu.VMEM(enc_weight.shape, BF16),
            pltpu.VMEM((n_mask, ch), BF16),
            pltpu.VMEM((n_mask, ch), BF16),
            pltpu.VMEM((2, rows, cols, ch), F32),
            pltpu.VMEM((2, 2, cols, ch), BF16),
            pltpu.VMEM((2, 2 * rows, ch), BF16),
            pltpu.VMEM((2, 2 * rows, ch), BF16),
            pltpu.VMEM((2, 16, ch), BF16),
            pltpu.VMEM((2, 16, ch), BF16),
            pltpu.VMEM((rows + 2 * BLOCK_ROWS, cols + 2 * BLOCK_COLS, ch), BF16),
            pltpu.VMEM((cb_n, rb_n * BLOCK, ch), BF16),
            pltpu.VMEM((cb_n, 9, UPSCALE * UPSCALE, rb_n * BLOCK), F32),
            pltpu.VMEM((rb_n + 2, cb_n + 2, 8, BLOCK), F32),
            pltpu.SemaphoreType.DMA((4,)),
            pltpu.SemaphoreType.DMA((34,)),
            pltpu.SemaphoreType.DMA((34,)),
        ],
        compiler_params=pltpu.CompilerParams(collective_id=0, has_side_effects=True),
        name="flow",
    )(frame_one, frame_two, enc_weight, mask_weight.T)


def solution(mesh):
    in_specs = (P("lat", "lon", None), P("lat", "lon", None), P(), P())
    out_specs = P(None, "lat", "lon")
    return jax.shard_map(body, mesh=mesh, in_specs=in_specs, out_specs=out_specs, check_vma=False)
```

```python
import functools
import math

import jax
import jax.numpy as jnp
from jax import lax
from jax.experimental import pallas as pl
from jax.experimental.pallas import tpu as pltpu
from jax.sharding import PartitionSpec as P

BLOCK_ROWS = 8
BLOCK_COLS = 16
BLOCK = BLOCK_ROWS * BLOCK_COLS
UPSCALE = 8
F32 = jnp.float32
BF16 = jnp.bfloat16
MESH = pl.DeviceIdType.MESH


def iota(shape, axis):
    return lax.broadcasted_iota(jnp.int32, shape, axis)


def mm(a, b):
    return jnp.dot(a, b, preferred_element_type=F32)


def mm_nt(a, b):
    return lax.dot_general(a, b, (((1,), (1,)), ((), ())), preferred_element_type=F32)


def swap_groups(xs, lane_group):
    xs = list(xs)
    for bit in (1, 2, 4):
        mask = (lane_group & bit) != 0
        shift = bit * BLOCK_COLS
        for a in range(8):
            if a & bit:
                continue
            lo, hi = xs[a], xs[a | bit]
            xs[a] = jnp.where(mask, pltpu.roll(hi, shift, 1), lo)
            xs[a | bit] = jnp.where(mask, hi, pltpu.roll(lo, BLOCK - shift, 1))
    return xs


def kernel(
    f1, f2, w_hbm, mw_hbm, out,
    fr, wv, mv, wp, acc, hal, strip_s, strip_r, corner_s, corner_r, keys, qs, mix, fb,
    lsem, ssem, rsem,
):
    rows, cols, ch = f1.shape
    rb_n, cb_n = rows // BLOCK_ROWS, cols // BLOCK_COLS
    n_mask = mw_hbm.shape[0]
    lat, lon = lax.axis_index("lat"), lax.axis_index("lon")
    nlat, nlon = lax.axis_size("lat"), lax.axis_size("lon")
    has_n, has_s = lat > 0, lat < nlat - 1
    left = (lat, lax.rem(lon + nlon - 1, nlon))
    right = (lat, lax.rem(lon + 1, nlon))
    north, south = (lat - 1, lon), (lat + 1, lon)

    loads = [
        pltpu.make_async_copy(f1, fr.at[0, pl.ds(1, rows)], lsem.at[0]),
        pltpu.make_async_copy(f2, fr.at[1, pl.ds(1, rows)], lsem.at[1]),
        pltpu.make_async_copy(w_hbm, wv, lsem.at[2]),
        pltpu.make_async_copy(mw_hbm, mv, lsem.at[3]),
    ]
    for load in loads:
        load.start()

    barrier = pltpu.get_barrier_semaphore()

    def greet(peer):
        pl.semaphore_signal(barrier, inc=1, device_id=peer, device_id_type=MESH)

    greet(left)
    greet(right)
    pl.when(has_n)(lambda: greet(north))
    pl.when(has_s)(lambda: greet(south))

    def send(k, src, dst, peer):
        return pltpu.make_async_remote_copy(
            src_ref=src, dst_ref=dst, send_sem=ssem.at[k], recv_sem=rsem.at[k],
            device_id=peer, device_id_type=MESH,
        )

    zero_row = jnp.zeros((cols, ch), BF16)
    for f in range(2):
        fr[f, 0] = zero_row
        fr[f, rows + 1] = zero_row

    halo_rows = {
        0: [send(0, f1.at[0], hal.at[1, 0], north), send(1, f2.at[0], hal.at[1, 1], north)],
        1: [
            send(2, f1.at[rows - 1], hal.at[0, 0], south),
            send(3, f2.at[rows - 1], hal.at[0, 1], south),
        ],
    }
    strips = [
        send(4, strip_s.at[0], strip_r.at[1], left),
        send(5, strip_s.at[1], strip_r.at[0], right),
    ]
    corners = [
        send(6, corner_s.at[0], corner_r.at[1], left),
        send(7, corner_s.at[1], corner_r.at[0], right),
    ]

    def absent(side):
        return jnp.logical_not(has_n if side == 0 else has_s)

    def present(side):
        return has_n if side == 0 else has_s

    for side in range(2):

        @pl.when(absent(side))
        def _():
            hal[side] = jnp.zeros(hal.shape[1:], hal.dtype)
            lo = 0 if side == 0 else BLOCK_ROWS + rows
            keys[lo : lo + BLOCK_ROWS] = jnp.zeros((BLOCK_ROWS,) + keys.shape[1:], BF16)
            at = 0 if side == 0 else rb_n + 1
            fb[at] = jnp.zeros(fb.shape[1:], F32)

    loads[0].wait()
    loads[1].wait()
    for side in range(2):
        lo, pick = (0, 0) if side == 0 else (cols - 16, 15)
        for f in range(2):
            tile = fr[f, 1 : rows + 1, lo : lo + 16, :].astype(F32)
            one = jnp.sum(jnp.where(iota(tile.shape, 1) == pick, tile, 0.0), axis=1)
            strip_s[side, f * rows : (f + 1) * rows] = one.astype(BF16)

    pl.semaphore_wait(barrier, 2 + has_n.astype(jnp.int32) + has_s.astype(jnp.int32))

    for side in range(2):

        @pl.when(present(side))
        def _():
            for copy in halo_rows[side]:
                copy.start()

    for copy in strips:
        copy.start()

    loads[2].wait()

    def col_shift(y, side):
        flat = y.reshape(-1, ch)
        n = flat.shape[0]
        turned = pltpu.roll(flat, 1 if side == 0 else n - 1, 0).reshape(y.shape)
        edge = 0 if side == 0 else cols - 1
        return jnp.where(iota(y.shape, 1) == edge, 0.0, turned)

    for f in range(2):
        lhs = jnp.concatenate(
            [fr[f, a : a + rows].reshape(rows * cols, ch) for a in range(3)], axis=1
        )
        ys = [mm(lhs, wv[:, b].reshape(3 * ch, ch)).reshape(rows, cols, ch) for b in range(3)]
        acc[f] = ys[1] + col_shift(ys[0], 0) + col_shift(ys[2], 1)

    for side in range(2):

        @pl.when(present(side))
        def _():
            for copy in halo_rows[1 - side]:
                copy.wait_recv()

    for side in range(2):
        edge = 0 if side == 0 else cols - 1
        base = 0 if side == 0 else cols - 16
        got = jnp.zeros((16, ch), F32)
        for f in range(2):
            for end in range(2):
                tile = hal[end, f, base : base + 16, :].astype(F32)
                one = tile[edge - base : edge - base + 1]
                got = jnp.where(iota((16, ch), 0) == 2 * f + end, one, got)
        corner_s[side] = got.astype(BF16)
    for copy in corners:
        copy.start()

    for side in range(2):
        a = 0 if side == 0 else 2
        r = 0 if side == 0 else rows - 1
        flat = hal[side].reshape(2 * cols, ch)
        ys = [mm(flat, wv[a, b]).reshape(2, cols, ch) for b in range(3)]
        y = ys[1] + col_shift(ys[0], 0) + col_shift(ys[2], 1)
        for f in range(2):
            acc[f, r] = acc[f, r] + y[f]

    br, bc = BLOCK_ROWS, BLOCK_COLS
    own_r = pl.ds(br, rows)
    edge_w = 8
    mid = (bc + edge_w, cols - 2 * edge_w)
    lows, highs = (bc, edge_w), (bc + cols - edge_w, edge_w)

    def key_row_sends(k, span, at=0, n=br):
        c = pl.ds(*span)
        return [
            send(k, keys.at[pl.ds(br + at, n), c], keys.at[pl.ds(br + rows + at, n), c], north),
            send(k + 1, keys.at[pl.ds(rows + at, n), c], keys.at[pl.ds(at, n), c], south),
        ]

    def key_col_sends(k, r, early):
        off = edge_w if early else 0
        back = 0 if early else edge_w
        return [
            send(k, keys.at[r, pl.ds(bc + off, edge_w)],
                 keys.at[r, pl.ds(bc + cols + off, edge_w)], left),
            send(k + 1, keys.at[r, pl.ds(cols + back, edge_w)],
                 keys.at[r, pl.ds(back, edge_w)], right),
        ]

    rows_mid = key_row_sends(8, mid)
    half = br // 2
    rows_edge = [
        [key_row_sends(10, lows, 0, half), key_row_sends(12, highs, 0, half)],
        [key_row_sends(34, lows, half, half), key_row_sends(36, highs, half, half)],
    ]
    cols_early = key_col_sends(14, own_r, True)
    cols_late = key_col_sends(24, own_r, False)
    corners_early, corners_late = {}, [{}, {}]
    for side in range(2):
        r = pl.ds(0 if side == 0 else br + rows, br)
        corners_early[side] = key_col_sends(26 + 4 * side, r, True)
        for part in range(2):
            r = pl.ds((0 if side == 0 else br + rows) + part * half, half)
            k = 28 + 4 * side if part == 0 else 38 + 2 * side
            corners_late[part][side] = key_col_sends(k, r, False)

    keys[br : br + rows, mid[0] : mid[0] + mid[1]] = acc[
        1, :, edge_w : cols - edge_w, :
    ].astype(BF16)
    for side in range(2):

        @pl.when(present(side))
        def _():
            rows_mid[side].start()

    for copy in cols_early:
        copy.start()

    loads[3].wait()
    p = iota((n_mask, n_mask), 0)
    want = (p - (p & 63)) + ((p & 7) << 3) + ((p >> 3) & 7)
    perm = (iota((n_mask, n_mask), 1) == want).astype(F32).astype(BF16)
    wp[...] = mm(perm, mv[...]).astype(BF16)

    for copy in strips + corners:
        copy.wait_recv()
    row_id = iota((rows, ch), 0)
    rims = []
    for side in range(2):
        lhs = jnp.concatenate([strip_r[side], corner_r[side]], axis=0)
        rims.append([mm(lhs, wv[a, 2 * side]) for a in range(3)])

    def add_rim_columns(f):
        for side in range(2):
            z = rims[side]
            own = [z[a][f * rows : (f + 1) * rows] for a in range(3)]
            top = z[0][2 * rows + 2 * f : 2 * rows + 2 * f + 1]
            bottom = z[2][2 * rows + 2 * f + 1 : 2 * rows + 2 * f + 2]
            h = own[1] + jnp.where(row_id == 0, top, pltpu.roll(own[0], 1, 0))
            h = h + jnp.where(row_id == rows - 1, bottom, pltpu.roll(own[2], rows - 1, 0))
            lo, pick = (0, 0) if side == 0 else (cols - 8, 7)
            tile = acc[f, :, lo : lo + 8, :]
            acc[f, :, lo : lo + 8, :] = tile + jnp.where(
                iota(tile.shape, 1) == pick, h[:, None, :], 0.0
            )

    add_rim_columns(1)
    for lo in (0, cols - edge_w):
        keys[br : br + rows, bc + lo : bc + lo + edge_w] = acc[
            1, :, lo : lo + edge_w, :
        ].astype(BF16)
    for side in range(2):

        @pl.when(present(side))
        def _():
            for part in rows_edge:
                for rows_sent in part:
                    rows_sent[side].start()

    for copy in cols_late:
        copy.start()

    add_rim_columns(0)

    for cb in range(cb_n):
        for rb in range(rb_n):
            block = acc[0, rb * br : (rb + 1) * br, cb * bc : (cb + 1) * bc, :]
            qs[cb, rb * BLOCK : (rb + 1) * BLOCK] = block.astype(BF16).reshape(BLOCK, ch)

    scale = 1.0 / math.sqrt(ch)
    inside = [has_n.astype(F32), has_s.astype(F32)]
    zero = jnp.zeros((8, BLOCK), F32)
    totals = {(rb, cb): [zero, zero, zero] for rb in range(rb_n) for cb in range(cb_n)}
    sub = iota((8, BLOCK), 0).astype(F32)

    def correlate(kbs, kc):
        part = keys[kbs[0] * br : (kbs[-1] + 1) * br, kc * bc : (kc + 1) * bc, :]
        part = part.reshape(len(kbs) * BLOCK, ch)
        for cb in range(max(0, kc - 2), min(cb_n, kc + 1)):
            rbs = [rb for rb in range(rb_n) if any(0 <= kb - rb <= 2 for kb in kbs)]
            r0 = rbs[0]
            s = mm_nt(part, qs[cb, r0 * BLOCK : (rbs[-1] + 1) * BLOCK])
            for at, kb in enumerate(kbs):
                for rb in rbs:
                    if not 0 <= kb - rb <= 2:
                        continue
                    e = s[at * BLOCK : (at + 1) * BLOCK, (rb - r0) * BLOCK : (rb - r0 + 1) * BLOCK]
                    e = jnp.exp(e * scale).reshape(br, 2, 8, BLOCK)
                    lanes = [e[:, h] for h in range(2)]
                    by_row = lanes[0] + lanes[1]
                    y = by_row[0] * float(br * (kb - rb - 1))
                    for kr in range(1, br):
                        y = y + by_row[kr] * float(br * (kb - rb - 1) + kr)
                    by_col = [jnp.sum(h, axis=0) for h in lanes]
                    m = by_col[0] + by_col[1]
                    off = float(bc * (kc - cb - 1))
                    x = by_col[0] * (sub + off) + by_col[1] * (sub + (off + 8.0))
                    if kb == 0 or kb == rb_n + 1:
                        gate = inside[0] if kb == 0 else inside[1]
                        m, y, x = m * gate, y * gate, x * gate
                    old = totals[rb, cb]
                    totals[rb, cb] = [old[0] + m, old[1] + y, old[2] + x]

    own_kbs = list(range(1, rb_n + 1))
    for kc in range(1, cb_n + 1):
        correlate(own_kbs, kc)

    def pass_on(arrivals, relays):
        for side in range(2):

            @pl.when(present(side))
            def _():
                for rows_sent in arrivals:
                    rows_sent[1 - side].wait_recv()
                for copy in relays[side]:
                    copy.start()

    pass_on([rows_mid], corners_early)

    for cb in range(cb_n):
        logits = mm_nt(wp[...], qs[cb]).reshape(9, UPSCALE * UPSCALE, rb_n * BLOCK)
        e = jnp.exp(logits)
        mix[cb] = e / jnp.sum(e, axis=0, keepdims=True)

    for part in range(2):
        pass_on(rows_edge[part], corners_late[part])

    for kc in range(1, cb_n + 1):
        correlate([0], kc)
        correlate([rb_n + 1], kc)
    for copy in cols_early + cols_late:
        copy.wait_recv()
    for kc in (0, cb_n + 1):
        correlate(own_kbs, kc)
    for side in range(2):

        @pl.when(present(side))
        def _():
            for copy in corners_early[side] + corners_late[0][side] + corners_late[1][side]:
                copy.wait_recv()

    for kc in (0, cb_n + 1):
        correlate([0], kc)
        correlate([rb_n + 1], kc)

    lane = iota((8, BLOCK), 1)
    sublane = iota((8, BLOCK), 0)
    qr, qc = lane >> 4, lane & 15
    for (rb, cb), (m, y, x) in totals.items():
        m, y, x = [jnp.sum(t, axis=0, keepdims=True) for t in (m, y, x)]
        fy = y / m - qr.astype(F32)
        fx = x / m - qc.astype(F32)
        both = jnp.where(sublane == 0, fy, fx) * float(UPSCALE)
        fb[rb + 1, cb + 1] = both

    flow_rows = [
        send(16, fb.at[1, pl.ds(1, cb_n)], fb.at[rb_n + 1, pl.ds(1, cb_n)], north),
        send(17, fb.at[rb_n, pl.ds(1, cb_n)], fb.at[0, pl.ds(1, cb_n)], south),
    ]
    flow_cols = [
        send(18, fb.at[pl.ds(1, rb_n), 1], fb.at[pl.ds(1, rb_n), cb_n + 1], left),
        send(19, fb.at[pl.ds(1, rb_n), cb_n], fb.at[pl.ds(1, rb_n), 0], right),
    ]
    flow_corners = {}
    for side in range(2):
        src_r, dst_r = (1, rb_n + 1) if side == 0 else (rb_n, 0)
        to = lat - 1 if side == 0 else lat + 1
        flow_corners[side] = [
            send(20 + 2 * side, fb.at[src_r, 1], fb.at[dst_r, cb_n + 1], (to, left[1])),
            send(21 + 2 * side, fb.at[src_r, cb_n], fb.at[dst_r, 0], (to, right[1])),
        ]
    for side in range(2):

        @pl.when(present(side))
        def _():
            for copy in flow_corners[side] + [flow_rows[side]]:
                copy.start()

    for copy in flow_cols:
        copy.start()
    for copy in flow_cols:
        copy.wait_recv()
    for side in range(2):

        @pl.when(present(side))
        def _():
            for copy in flow_corners[1 - side] + [flow_rows[1 - side]]:
                copy.wait_recv()

    k = iota((BLOCK, BLOCK), 0)
    weave = (iota((BLOCK, BLOCK), 1) == ((k & 15) << 3) + (k >> 4)).astype(F32).astype(BF16)

    for cb in range(cb_n):
        for rb in range(rb_n):
            shifted = {}
            for r in range(rb, rb + 3):
                mid = fb[r, cb + 1]
                shifted[r, 0] = jnp.where(
                    qc == 0, pltpu.roll(fb[r, cb], BLOCK - 15, 1), pltpu.roll(mid, 1, 1)
                )
                shifted[r, 1] = mid
                shifted[r, 2] = jnp.where(
                    qc == 15, pltpu.roll(fb[r, cb + 2], 15, 1), pltpu.roll(mid, BLOCK - 1, 1)
                )
            beside = []
            for a in range(3):
                for b in range(3):
                    here = shifted[rb + 1, b]
                    if a == 0:
                        here = pltpu.roll(jnp.where(qr == 7, shifted[rb, b], here), bc, 1)
                    if a == 2:
                        here = pltpu.roll(
                            jnp.where(qr == 0, shifted[rb + 2, b], here), BLOCK - bc, 1
                        )
                    beside.append(here)
            for d in range(2):
                up = jnp.zeros((UPSCALE * UPSCALE, BLOCK), F32)
                for n in range(9):
                    share = mix[cb, n, :, rb * BLOCK : (rb + 1) * BLOCK]
                    up = up + share * beside[n][d : d + 1]
                xs = [up[8 * j : 8 * j + 8] for j in range(8)]
                rowed = jnp.concatenate(swap_groups(xs, qr), axis=0)
                high = rowed.astype(BF16)
                rest = rowed - high.astype(F32)
                mid = rest.astype(BF16)
                low = (rest - mid.astype(F32)).astype(BF16)
                woven = mm(high, weave) + mm(mid, weave) + mm(low, weave)
                out[d, rb * 64 : (rb + 1) * 64, cb * BLOCK : (cb + 1) * BLOCK] = woven

    for side in range(2):

        @pl.when(present(side))
        def _():
            for copy in halo_rows[side] + [
                rows_mid[side], flow_rows[side]
            ] + [sent[side] for part in rows_edge for sent in part]:
                copy.wait_send()
            for copy in corners_early[side] + corners_late[0][side] + corners_late[1][side] + flow_corners[side]:
                copy.wait_send()

    for copy in strips + corners + cols_early + cols_late + flow_cols:
        copy.wait_send()


def body(frame_one, frame_two, enc_weight, mask_weight):
    rows, cols, ch = frame_one.shape
    n_mask = mask_weight.shape[1]
    rb_n, cb_n = rows // BLOCK_ROWS, cols // BLOCK_COLS
    return pl.pallas_call(
        kernel,
        out_shape=jax.ShapeDtypeStruct((2, rows * UPSCALE, cols * UPSCALE), F32),
        in_specs=[pl.BlockSpec(memory_space=pl.ANY)] * 4,
        out_specs=pl.BlockSpec(memory_space=pltpu.VMEM),
        scratch_shapes=[
            pltpu.VMEM((2, rows + 2, cols, ch), BF16),
            pltpu.VMEM(enc_weight.shape, BF16),
            pltpu.VMEM((n_mask, ch), BF16),
            pltpu.VMEM((n_mask, ch), BF16),
            pltpu.VMEM((2, rows, cols, ch), F32),
            pltpu.VMEM((2, 2, cols, ch), BF16),
            pltpu.VMEM((2, 2 * rows, ch), BF16),
            pltpu.VMEM((2, 2 * rows, ch), BF16),
            pltpu.VMEM((2, 16, ch), BF16),
            pltpu.VMEM((2, 16, ch), BF16),
            pltpu.VMEM((rows + 2 * BLOCK_ROWS, cols + 2 * BLOCK_COLS, ch), BF16),
            pltpu.VMEM((cb_n, rb_n * BLOCK, ch), BF16),
            pltpu.VMEM((cb_n, 9, UPSCALE * UPSCALE, rb_n * BLOCK), F32),
            pltpu.VMEM((rb_n + 2, cb_n + 2, 8, BLOCK), F32),
            pltpu.SemaphoreType.DMA((4,)),
            pltpu.SemaphoreType.DMA((42,)),
            pltpu.SemaphoreType.DMA((42,)),
        ],
        compiler_params=pltpu.CompilerParams(collective_id=0, has_side_effects=True),
        name="flow",
    )(frame_one, frame_two, enc_weight, mask_weight.T)


def solution(mesh):
    in_specs = (P("lat", "lon", None), P("lat", "lon", None), P(), P())
    out_specs = P(None, "lat", "lon")
    return jax.shard_map(body, mesh=mesh, in_specs=in_specs, out_specs=out_specs, check_vma=False)
```
